256 devices in a mesh: blk: 128 (over x, y, z), head: 2 (over core).
Axes of the slice: x: 4, y: 4, z: 8, core: 2. Of those that a mesh axis runs over, the one named last changes fastest.
Arguments:
- features: bfloat16 [131072, 512], P('blk')
- w_qkv: bfloat16 [3, 512, 512], P(None, None, 'head'), may hold values from -0.25 to 0.25
- w_out: bfloat16 [512, 512], P('head'), may hold values from -0.25 to 0.25
- key_lists: int32 [512, 16], P('blk'), may hold values from 0 to 511, as said below
- key_counts: int32 [512], P('blk'), may hold values from 2 to 16
- node_mask: int32 [131072], replicated, may hold values from 0 to 1, as said below
- hub_ids: int32 [8], replicated, may hold values from 0 to 511, as said below
Outputs:
- mixed: bfloat16 [131072, 512], P('blk', 'head')
The draws below stay inside these ranges and needn't reach their ends.
Inputs may be any that keep to these rules, and one draw needn't show every extreme that they name: `key_lists`: in row b, entry 0 is b; entries 1 to 4 are positions in hub_ids (0 to 7); every other entry is a block within 2 blocks of b. `node_mask`: the first node of every block is 1. `hub_ids`: distinct block numbers.
All inputs are finite; a program needn't handle non-finite values.
Results may differ from the reference program's by a relative error of at most 0.0034.
The reference program's roundings to bfloat16 on the way (of `weight` and `attended`) count: a program that leaves them out, or rounds other values in their place, can miss the bound.
Values may be sent and summed in bfloat16 or wider, within the bound.
A program may use at most 64 MiB of HBM per device.

```python
import jax
import jax.numpy as jnp
from jax import lax

D = 512
HEADS = 8
DH = 64
B = 256
REACH = 2
KL = 16
KL_HUB = 4
HUBS = 8
NB = 512
NODES = 131072


def hub_table(key):
    inner = jax.random.permutation(jax.random.fold_in(key, 11), NB - 2)[:HUBS - 2].astype(jnp.int32) + 1
    ends = jnp.array([0, NB - 1], dtype=jnp.int32)
    joined = jnp.concatenate([ends, inner]).astype(jnp.int32)
    return jax.random.permutation(jax.random.fold_in(key, 17), joined).astype(jnp.int32)


def draw_features(key, part):
    base = jnp.clip(jax.random.normal(key, (NODES, D), jnp.float32), -6.0, 6.0)
    return base.astype(jnp.bfloat16)


def draw_node_mask(key, part):
    marks = (jax.random.randint(key, (NB, B), 0, 4) > 0).astype(jnp.int32)
    marks = marks.at[:, 0].set(1)
    return marks.reshape(NODES)


def draw_hub_ids(key, part):
    return hub_table(key)


def draw_key_lists(key, part):
    own = jnp.arange(NB, dtype=jnp.int32)[:, None]
    slots = jax.random.randint(jax.random.fold_in(key, 12), (NB, KL_HUB), 0, HUBS)
    offsets = jax.random.randint(jax.random.fold_in(key, 13), (NB, KL - 1 - KL_HUB), -REACH, REACH + 1)
    near = jnp.clip(own + offsets, 0, NB - 1)
    return jnp.concatenate([own, slots, near], axis=1).astype(jnp.int32)


def draw_key_counts(key, part):
    base = jax.random.fold_in(key, 21)
    counts = jax.random.randint(base, (NB,), 2, KL + 1)
    first = jax.random.randint(jax.random.fold_in(base, 1), (), 0, NB)
    second = (first + 1 + jax.random.randint(jax.random.fold_in(base, 2), (), 0, NB - 1)) % NB
    counts = counts.at[first].set(KL)
    counts = counts.at[second].set(2)
    return counts.astype(jnp.int32)


def levels(key, shape, shards, least, high):
    def one(axis_at, parts):
        steps = jax.random.uniform(jax.random.fold_in(jax.random.fold_in(key, 6), axis_at), (parts,), jnp.float32, least / len(shards), high / len(shards))
        return jnp.repeat(jnp.exp(steps), shape[axis_at] // parts).reshape((-1,) + (1,) * (len(shape) - axis_at - 1))

    level = one(*shards[0])
    for cut in shards[1:]:
        level = level * one(*cut)
    return level


def centred(own_key, extent, deviation, limit, shards=(), kind=jnp.bfloat16):
    drawn = jax.random.normal(own_key, extent, jnp.float32) * deviation
    if len(shards) > 0:
        drawn = levels(own_key, extent, shards, -0.22, 0.18) * drawn
    return jnp.clip(drawn, min=-limit, max=limit).astype(kind)


def setup_inputs(seed: int = 0) -> dict:
    splits = jax.random.split(jax.random.key(seed), 8)
    return {
        "features": draw_features(jax.random.fold_in(splits[7], 71), 0),
        "w_qkv": centred(splits[1], (3, D, D), D ** -0.5, 0.25, ((2, 2),)),
        "w_out": centred(splits[2], (D, D), D ** -0.5, 0.25, ((0, 2),)),
        "key_lists": draw_key_lists(jax.random.fold_in(splits[7], 71), 0),
        "key_counts": draw_key_counts(jax.random.fold_in(splits[7], 71), 0),
        "node_mask": draw_node_mask(jax.random.fold_in(splits[7], 71), 0),
        "hub_ids": draw_hub_ids(jax.random.fold_in(splits[7], 71), 0),
    }


def reference(features, w_qkv, w_out, key_lists, key_counts, node_mask, hub_ids):
    query = jnp.dot(features, w_qkv[0], preferred_element_type=jnp.float32).astype(jnp.bfloat16)
    keys = jnp.dot(features, w_qkv[1], preferred_element_type=jnp.float32).astype(jnp.bfloat16)
    values = jnp.dot(features, w_qkv[2], preferred_element_type=jnp.float32).astype(jnp.bfloat16)
    query = query.reshape(NB, B, HEADS, DH)
    keys = keys.reshape(NB, B, HEADS, DH)
    values = values.reshape(NB, B, HEADS, DH)
    masks = node_mask.reshape(NB, B)
    column = jnp.arange(KL, dtype=jnp.int32)
    is_hub = (column >= 1) & (column <= KL_HUB)
    scale = float(DH) ** -0.5

    def one_block(b):
        entries = key_lists[b]
        slots = jnp.clip(entries, 0, HUBS - 1).astype(jnp.int32)
        target = jnp.where(is_hub, hub_ids[slots], entries).astype(jnp.int32)
        live = column < key_counts[b]
        valid = (masks[target] > 0) & live[:, None]
        valid = valid.reshape(KL * B)
        block_keys = keys[target].reshape(KL * B, HEADS, DH).astype(jnp.float32)
        block_vals = values[target].reshape(KL * B, HEADS, DH).astype(jnp.float32)
        qrows = query[b].astype(jnp.float32)
        score = jnp.einsum("qhd,khd->hqk", qrows, block_keys) * scale
        score = jnp.where(valid[None, None, :], score, jnp.float32(-1e30))
        top = jnp.max(score, axis=2, keepdims=True)
        expo = jnp.where(valid[None, None, :], jnp.exp(score - top), jnp.float32(0.0))
        total = jnp.sum(expo, axis=2)
        weight = expo.astype(jnp.bfloat16).astype(jnp.float32)
        summed = jnp.einsum("hqk,khd->qhd", weight, block_vals)
        attended = summed / jnp.transpose(total)[:, :, None]
        return attended.reshape(B, D).astype(jnp.bfloat16)

    attended = lax.map(one_block, jnp.arange(NB, dtype=jnp.int32)).reshape(NODES, D)
    mixed = jnp.dot(attended, w_out, preferred_element_type=jnp.float32) + features.astype(jnp.float32)
    return mixed.astype(jnp.bfloat16)
```

```python
import functools

import jax
import jax.numpy as jnp
from jax import lax
from jax.experimental import pallas as pl
from jax.experimental.pallas import tpu as pltpu
from jax.sharding import PartitionSpec as P

F32 = jnp.float32
BF16 = jnp.bfloat16
HEADS_HERE, DH, B = 4, 64, 256
NT = (((1,), (1,)), ((), ()))
LIMIT = 2.0e5
NEG = -1e30


def attn_kernel(mode, first_of, lists, counts, hub_ids, feat, hubs, halo, w_qkv, mask, out,
                qpad, keys, vals, bias, acc, top, att_t, cnt):
    first = first_of() * 4
    for b in range(4):
        for i in range(16):
            cnt[b, i] = 0
    for b in range(4):
        for j in range(16):
            entry = lists[b, j]
            if 1 <= j <= 4:
                at = 8 + entry
            else:
                at = entry - first + 2
            cnt[b, at] += jnp.where(j < counts[b], 1, 0)

    wq, wk = w_qkv[0], w_qkv[1]
    wv_t = w_qkv[2].T
    lane_head = lax.broadcasted_iota(jnp.int32, (256, 256), 1) // DH
    sums = (lax.broadcasted_iota(jnp.int32, (256, 128), 0) // DH
            == lax.broadcasted_iota(jnp.int32, (256, 128), 1)).astype(BF16)

    def most(rows):
        sq = rows.astype(F32)
        sq = (sq * sq).astype(BF16)
        return jnp.max(jnp.dot(sq, sums, preferred_element_type=F32), axis=0, keepdims=True)

    qn = jnp.zeros((1, 128), F32)
    for b in range(4):
        q = jnp.dot(feat[b * B:(b + 1) * B, :], wq, preferred_element_type=F32).astype(BF16)
        qn = jnp.maximum(qn, most(q))
        q = q * jnp.asarray(DH ** -0.5, BF16)
        for h in range(HEADS_HERE):
            qpad[b, h * B:(h + 1) * B, :] = jnp.where(lane_head == h, q, jnp.zeros_like(q))

    def block_rows(i):
        if i < 2:
            return halo[0, 0, i], halo[1, 0, i]
        if i < 6:
            own = feat[(i - 2) * B:(i - 1) * B, :]
            return own[:, :256], own[:, 256:]
        if i < 8:
            return halo[0, 1, i - 6], halo[1, 1, i - 6]
        k = i - 8
        left = jnp.concatenate([hubs[0, x, y, k] for x in range(4) for y in range(4)], axis=0)
        right = jnp.concatenate([hubs[1, y, x, k] for x in range(4) for y in range(4)], axis=0)
        return left, right

    kn = jnp.zeros((1, 128), F32)
    for i in range(16):
        r0, r1 = block_rows(i)
        if i < 2 or 6 <= i < 8:
            r0 = r0.reshape(B, 256)
            r1 = r1.reshape(B, 256)
        rows = jnp.concatenate([r0, r1], axis=1)
        k = jnp.dot(rows, wk, preferred_element_type=F32).astype(BF16)
        keys[i] = k
        kn = jnp.maximum(kn, most(k))
        if i < 8:
            node = jnp.clip(first + (i - 2), 0, mask.shape[0] - 1)
        else:
            node = hub_ids[i - 8]
        usable = mask[pl.ds(node, 1), :]
        usable = (usable > 0).astype(F32)
        v_t = lax.dot_general(wv_t, rows, NT, preferred_element_type=F32).astype(BF16)
        v_t = v_t * usable.astype(BF16)
        tail = jnp.concatenate([usable, jnp.zeros((15, 256), F32)], axis=0).astype(BF16)
        for h in range(HEADS_HERE):
            vals[i, h, 0:DH, :] = v_t[h * DH:(h + 1) * DH, :]
            vals[i, h, DH:DH + 16, :] = tail
        off = jnp.broadcast_to((usable - 1.0) * 1e30, (128, 256))
        bias[i] = off.T

    safe = jnp.max(qn) * jnp.max(kn) <= LIMIT

    def run(fast):
        @pl.loop(0, 4)
        def _(b):
            acc[...] = jnp.zeros_like(acc)
            if not fast:
                top[...] = jnp.full_like(top, NEG)

            @pl.loop(0, 13)
            def _(t):
                at = jnp.where(t < 5, b + t, t + 3)
                times = cnt[b, at]

                @pl.when(times > 0)
                def _():
                    scale = times.astype(F32)
                    kb = keys[at]
                    for h in range(HEADS_HERE):
                        s = lax.dot_general(kb, qpad[b, h * B:(h + 1) * B, :], NT,
                                            preferred_element_type=F32)
                        if fast:
                            p = jnp.exp(s).astype(BF16)
                            acc[h] += scale * jnp.dot(vals[at, h], p, preferred_element_type=F32)
                        else:
                            low = bias[at]
                            s = s + jnp.concatenate([low, low], axis=1)
                            old = top[h]
                            new = jnp.maximum(old, jnp.max(s, axis=0, keepdims=True))
                            top[h] = new
                            p = jnp.exp(s - new).astype(BF16)
                            acc[h] = jnp.exp(old - new) * acc[h] + scale * jnp.dot(
                                vals[at, h], p, preferred_element_type=F32)

            for h in range(HEADS_HERE):
                att_t[h * DH:(h + 1) * DH, :] = (acc[h, 0:DH, :] / acc[h, DH:DH + 1, :]).astype(BF16)
            out[pl.ds(pl.multiple_of(b * B, B), B), :] = att_t[...].T

    if mode == "both":
        @pl.when(safe)
        def _():
            run(True)

        @pl.when(jnp.logical_not(safe))
        def _():
            run(False)
    else:
        run(mode == "fast")


def attention(first_of, lists, counts, hub_ids, feat, hubs, halo, w_qkv, mask, mode="both"):
    smem = pl.BlockSpec(memory_space=pltpu.SMEM)
    vmem = pl.BlockSpec(memory_space=pltpu.VMEM)
    return pl.pallas_call(
        functools.partial(attn_kernel, mode, first_of),
        out_shape=jax.ShapeDtypeStruct((1024, 256), BF16),
        in_specs=[smem, smem, smem, vmem, vmem, vmem, vmem, vmem],
        out_specs=vmem,
        scratch_shapes=[
            pltpu.VMEM((4, 1024, 256), BF16),
            pltpu.VMEM((16, 256, 256), BF16),
            pltpu.VMEM((16, 4, 80, 256), BF16),
            pltpu.VMEM((16, 256, 128), F32),
            pltpu.VMEM((4, 80, 256), F32),
            pltpu.VMEM((4, 1, 256), F32),
            pltpu.VMEM((256, 256), BF16),
            pltpu.SMEM((4, 16), jnp.int32),
        ],
        compiler_params=pltpu.CompilerParams(vmem_limit_bytes=48 << 20),
        name="attention",
    )(lists, counts, hub_ids, feat, hubs, halo, w_qkv, mask)


MESH = pl.DeviceIdType.MESH


def comm_kernel(hub_ids, feat, hubs, halo, plane, zsend, zrecv, local,
                p_send, p_recv, z_send, z_recv, g_send, g_recv, a_send, a_recv,
                b_send, b_recv, c_send, c_recv, n_send, n_recv):
    me = lax.axis_index("blk")
    core = lax.axis_index("head")
    devices = lax.axis_size("blk")
    x, y, z = me // 32, (me // 8) % 4, me % 8
    a = jnp.where(core == 0, y, x)
    b = jnp.where(core == 0, x, y)
    step_a = jnp.where(core == 0, 8, 32)
    step_b = jnp.where(core == 0, 32, 8)
    columns = pl.ds(pl.multiple_of(core * 256, 256), 256)
    other = 1 - core
    after = (me + 1) % devices
    before = (me + devices - 1) % devices

    def at_plane(k):
        xx, yy = (x + k // 4) % 4, (y + k % 4) % 4
        return xx * 4 + yy, xx * 32 + yy * 8 + z

    def at_line(k):
        zz = (z + k) % 8
        return zz, x * 32 + y * 8 + zz

    def remote(src, dst, send, recv, blk, head):
        return pltpu.make_async_remote_copy(src_ref=src, dst_ref=dst, send_sem=send, recv_sem=recv,
                                            device_id=(blk, head), device_id_type=MESH)

    barrier = pltpu.get_barrier_semaphore()

    def greet(blk, head):
        pl.semaphore_signal(barrier, inc=1, device_id=(blk, head), device_id_type=MESH)

    for k in range(1, 16):
        greet(at_plane(k)[1], core)
    for k in range(1, 8):
        greet(at_line(k)[1], core)
    greet(me, other)
    greet(after, core)
    greet(before, core)
    mine = x * 4 + y
    own = pltpu.make_async_copy(feat.at[:, mine, :, columns], plane.at[mine], local)
    own.start()
    pl.semaphore_wait(barrier, 25)

    first = []
    for k in range(1, 16):
        part, blk = at_plane(k)
        first.append(remote(feat.at[:, part, :, columns], plane.at[mine],
                            p_send.at[k - 1], p_recv.at[k - 1], blk, core))
        first[-1].start()
    near = [
        remote(feat.at[2:4, :, :, columns], halo.at[core, 0], n_send.at[0], n_recv.at[0], after, core),
        remote(feat.at[0:2, :, :, columns], halo.at[core, 1], n_send.at[1], n_recv.at[1], before, core),
    ]
    for copy in near:
        copy.start()
    own.wait()
    for copy in first:
        copy.wait_recv()

    for k in range(8):
        h = hub_ids[k]
        zsend[k] = plane[lax.div(h, 32), lax.rem(h, 4)]
    second = []
    for k in range(1, 8):
        zz, blk = at_line(k)
        second.append(remote(zsend.at[zz], zrecv.at[z], z_send.at[k - 1], z_recv.at[k - 1], blk, core))
        second[-1].start()
    zrecv[z] = zsend[z]
    for copy in second:
        copy.wait_recv()

    hubs[core, b, a, z] = zrecv[lax.rem(lax.div(hub_ids[z], 4), 8)]
    third = []
    for k in range(1, 8):
        zz, blk = at_line(k)
        third.append(remote(hubs.at[core, b, a, z], hubs.at[core, b, a, z],
                            g_send.at[k - 1], g_recv.at[k - 1], blk, core))
        third[-1].start()
    for copy in third:
        copy.wait_recv()

    fourth = []
    for k in range(1, 4):
        fourth.append(remote(hubs.at[core, b, a], hubs.at[core, b, a], a_send.at[k - 1], a_recv.at[k - 1],
                             me + ((a + k) % 4 - a) * step_a, core))
        fourth[-1].start()
    for copy in fourth:
        copy.wait_recv()

    up, down, far = (b + 1) % 4, (b + 3) % 4, (b + 2) % 4
    up_blk = me + (up - b) * step_b
    down_blk = me + (down - b) * step_b

    def slab(i, n):
        return remote(hubs.at[core, i], hubs.at[core, i], c_send.at[n], c_recv.at[n], me, other)

    fifth = [
        remote(hubs.at[core, b], hubs.at[core, b], b_send.at[0], b_recv.at[0], up_blk, core),
        remote(hubs.at[core, b], hubs.at[core, b], b_send.at[1], b_recv.at[1], down_blk, core),
    ]
    for copy in fifth:
        copy.start()
    pair = [slab(b, 0)]
    pair[0].start()
    fifth[0].wait_recv()
    fifth.append(remote(hubs.at[core, down, 0:2], hubs.at[core, down, 0:2], b_send.at[2], b_recv.at[2],
                        up_blk, core))
    fifth[2].start()
    fifth[1].wait_recv()
    fifth.append(remote(hubs.at[core, up, 2:4], hubs.at[core, up, 2:4], b_send.at[3], b_recv.at[3],
                        down_blk, core))
    fifth[3].start()
    pair.append(slab(down, 1))
    pair[1].start()
    pair.append(slab(up, 2))
    pair[2].start()
    for i in range(2):
        near[i].wait_recv()
        pair.append(remote(halo.at[core, i], halo.at[core, i], c_send.at[4 + i], c_recv.at[4 + i], me, other))
        pair[-1].start()
    fifth[2].wait_recv()
    fifth[3].wait_recv()
    pair.append(slab(far, 3))
    pair[-1].start()

    for copy in first + near + second + third + fourth + fifth:
        copy.wait_send()
    for copy in pair:
        copy.wait()


def exchange(hub_ids, feat):
    dma = pltpu.SemaphoreType.DMA
    return pl.pallas_call(
        comm_kernel,
        out_shape=(jax.ShapeDtypeStruct((2, 4, 4, 8, 16, 256), BF16),
                   jax.ShapeDtypeStruct((2, 2, 2, 16, 16, 256), BF16)),
        in_specs=[pl.BlockSpec(memory_space=pltpu.SMEM), pl.BlockSpec(memory_space=pltpu.VMEM)],
        out_specs=(pl.BlockSpec(memory_space=pltpu.VMEM), pl.BlockSpec(memory_space=pltpu.VMEM)),
        scratch_shapes=[
            pltpu.VMEM((16, 4, 16, 256), BF16),
            pltpu.VMEM((8, 16, 256), BF16),
            pltpu.VMEM((8, 16, 256), BF16),
            dma(()),
            dma((15,)), dma((15,)), dma((7,)), dma((7,)), dma((7,)), dma((7,)), dma((3,)), dma((3,)),
            dma((4,)), dma((4,)), dma((6,)), dma((6,)), dma((2,)), dma((2,)),
        ],
        compiler_params=pltpu.CompilerParams(collective_id=0, has_side_effects=True,
                                             vmem_limit_bytes=32 << 20),
        name="exchange",
    )(hub_ids, feat.reshape(4, 16, 16, 512))


def body(features, w_qkv, w_out, key_lists, key_counts, node_mask, hub_ids):
    rows, width = features.shape
    local = w_qkv.shape[2]
    me = lax.axis_index("head")
    swap = [(0, 1), (1, 0)]
    share = width // 2
    w_mine = lax.dynamic_slice_in_dim(w_out, me * share, share, 1)
    w_sent = lax.dynamic_slice_in_dim(w_out, (1 - me) * share, share, 1)
    w_got = lax.ppermute(w_sent, "head", swap)
    hubs, halo = exchange(hub_ids, features)
    attended = attention(lambda: lax.axis_index("blk"), key_lists, key_counts, hub_ids, features,
                         hubs, halo, w_qkv, node_mask.reshape(-1, B))
    theirs = lax.ppermute(attended, "head", swap)
    resid = lax.dynamic_slice_in_dim(features, me * share, share, 1)
    mixed = (jnp.dot(attended, w_mine, preferred_element_type=F32)
             + jnp.dot(theirs, w_got, preferred_element_type=F32) + resid.astype(F32))
    return mixed.astype(BF16)


def solution(mesh):
    placed = (P("blk", None), P(None, None, "head"), P("head", None), P("blk", None), P("blk"), P(), P())
    return jax.shard_map(body, mesh=mesh, in_specs=placed, out_specs=P("blk", "head"), check_vma=False)
```

```python
import functools

import jax
import jax.numpy as jnp
from jax import lax
from jax.experimental import pallas as pl
from jax.experimental.pallas import tpu as pltpu
from jax.sharding import PartitionSpec as P

F32 = jnp.float32
BF16 = jnp.bfloat16
HEADS_HERE, DH, B = 4, 64, 256
TALL = DH + 16
NT = (((1,), (1,)), ((), ()))
NEG = -1e30
MESH = pl.DeviceIdType.MESH
VMEM = pl.BlockSpec(memory_space=pltpu.VMEM)
SMEM = pl.BlockSpec(memory_space=pltpu.SMEM)
ORDER = sorted(range(1, 16), key=lambda k: -(min(k // 4, 4 - k // 4) + min(k % 4, 4 - k % 4)))


def project(rows, wk, wv_t, usable, keys, vals, bias, i):
    keys[i] = jnp.dot(rows, wk, preferred_element_type=F32).astype(BF16)
    v_t = lax.dot_general(wv_t, rows, NT, preferred_element_type=F32).astype(BF16)
    tail = jnp.concatenate([usable, jnp.zeros((TALL - DH - 1, B), F32)], axis=0).astype(BF16)
    for h in range(HEADS_HERE):
        vals[i, h, 0:DH, :] = v_t[h * DH:(h + 1) * DH, :] * usable.astype(BF16)
        vals[i, h, DH:TALL, :] = tail
    bias[i] = jnp.broadcast_to((usable - 1.0) * 1e30, (128, B)).T


def attend(q_t, b, kb, vb, low, times, acc, top):
    low = low + jnp.where(times > 0, 0.0, NEG)
    low = jnp.concatenate([low, low], axis=1)
    scale = times.astype(F32)
    heads = range(HEADS_HERE)
    ss = [jnp.dot(kb, q_t[b, h], preferred_element_type=F32) for h in heads]
    ss = [s + low for s in ss]
    olds = [top[b, h] for h in heads]
    news = [jnp.maximum(o, jnp.max(s, axis=0, keepdims=True)) for o, s in zip(olds, ss)]
    ps = [jnp.exp(s - n).astype(BF16) for s, n in zip(ss, news)]
    got = [jnp.dot(vb[h], ps[h], preferred_element_type=F32) for h in heads]
    for h in heads:
        acc[b, h] = jnp.exp(olds[h] - news[h]) * acc[b, h] + scale * got[h]
        top[b, h] = news[h]


def near_kernel(hub_ids, lists, counts, feat, w_qkv, mask, hubs, q_t, acc, top,
                halo, plane, zsend, zrecv, wv_t, keys, vals, bias, local,
                p_send, p_recv, z_send, z_recv, g_send, g_recv, a_send, a_recv,
                c_send, c_recv, n_send, n_recv, m_send, m_recv):
    me = lax.axis_index("blk")
    core = lax.axis_index("head")
    devices = lax.axis_size("blk")
    x, y, z = me // 32, (me // 8) % 4, me % 8
    mine = x * 4 + y
    columns = pl.ds(pl.multiple_of(core * 256, 256), 256)
    other = 1 - core
    after = (me + 1) % devices
    before = (me + devices - 1) % devices

    def at_plane(k, sign=1):
        xx, yy = (x + sign * (k // 4) + 4) % 4, (y + sign * (k % 4) + 4) % 4
        return xx * 4 + yy, xx * 32 + yy * 8 + z

    def at_line(k):
        zz = (z + k) % 8
        return zz, x * 32 + y * 8 + zz

    def remote(src, dst, send, recv, blk, head):
        return pltpu.make_async_remote_copy(src_ref=src, dst_ref=dst, send_sem=send, recv_sem=recv,
                                            device_id=(blk, head), device_id_type=MESH)

    barrier = pltpu.get_barrier_semaphore()

    def greet(blk, head):
        pl.semaphore_signal(barrier, inc=1, device_id=(blk, head), device_id_type=MESH)

    for k in ORDER:
        greet(at_plane(k)[1], core)
    for k in range(1, 8):
        greet(at_line(k)[1], core)
    greet(after, core)
    greet(before, core)
    greet(me, other)
    own = pltpu.make_async_copy(feat.at[:, mine, :, columns], plane.at[mine], local)
    own.start()

    first = me * 4
    wv_t[...] = w_qkv[2].T
    row_head = lax.broadcasted_iota(jnp.int32, (B, B), 0) // DH
    acc[...] = jnp.zeros_like(acc)
    top[...] = jnp.full_like(top, NEG)

    def usable_of(node):
        return (mask[pl.ds(node, 1), :] > 0).astype(F32)

    @pl.loop(0, 4)
    def _(b):
        rows = feat[b].reshape(B, 512)
        q = jnp.dot(rows, w_qkv[0], preferred_element_type=F32).astype(BF16)
        q = (q * jnp.asarray(DH ** -0.5, BF16)).T
        for h in range(HEADS_HERE):
            q_t[b, h] = jnp.where(row_head == h, q, jnp.zeros_like(q))
        project(rows, w_qkv[1], wv_t[...], usable_of(first + b), keys, vals, bias, b + 2)

    def meet(b, i):
        times = jnp.int32(0)
        for j in [0] + list(range(5, 16)):
            hit = (lists[b, j] == first + i - 2) & (j < counts[b])
            times = times + jnp.where(hit, 1, 0)
        attend(q_t, b, keys[i], vals.at[i], bias[i], times, acc, top)

    pl.semaphore_wait(barrier, 25)

    scatter = {}
    for k in ORDER:
        part, blk = at_plane(k)
        scatter[k] = remote(feat.at[:, part, :, columns], plane.at[mine],
                            p_send.at[k - 1], p_recv.at[k - 1], blk, core)
        scatter[k].start()

    @pl.loop(0, 10)
    def _(n):
        b = (n + 1) // 3
        meet(b, b + 1 + (n + 1) % 3)

    own.wait()
    for copy in scatter.values():
        copy.wait_recv()

    for k in range(8):
        zsend[k] = plane[lax.div(hub_ids[k], 32), lax.rem(hub_ids[k], 4)]
    lines = []
    for k in (4, 3, 5, 2, 6, 1, 7):
        zz, blk = at_line(k)
        lines.append(remote(zsend.at[zz], zrecv.at[z], z_send.at[k - 1], z_recv.at[k - 1], blk, core))
        lines[-1].start()
    zrecv[z] = zsend[z]

    @pl.loop(0, 4)
    def _(n):
        b = (n % 2) * 2 + n // 2
        meet(b, (b + 2) % 4 + 2)

    for copy in lines:
        copy.wait_recv()
    hubs[core, mine, z] = zrecv[lax.rem(lax.div(hub_ids[z], 4), 8)]
    spread = []
    for k in (4, 3, 5, 2, 6, 1, 7):
        zz, blk = at_line(k)
        spread.append(remote(hubs.at[core, mine, z], hubs.at[core, mine, z],
                             g_send.at[k - 1], g_recv.at[k - 1], blk, core))
        spread[-1].start()
    for copy in spread:
        copy.wait_recv()

    gather = {}
    for k in ORDER:
        gather[k] = remote(hubs.at[core, mine], hubs.at[core, mine], a_send.at[k - 1], a_recv.at[k - 1],
                           at_plane(k)[1], core)
        gather[k].start()
    near = [
        remote(feat.at[2:4, :, :, columns], halo.at[core, 0], n_send.at[0], n_recv.at[0], after, core),
        remote(feat.at[0:2, :, :, columns], halo.at[core, 1], n_send.at[1], n_recv.at[1], before, core),
    ]
    for copy in near:
        copy.start()
    pair = [remote(hubs.at[core, mine], hubs.at[core, mine], c_send.at[0], c_recv.at[0], me, other)]
    pair[0].start()
    twin = []
    for i in range(2):
        near[i].wait_recv()
        twin.append(remote(halo.at[core, i], halo.at[core, i], m_send.at[i], m_recv.at[i], me, other))
        twin[i].start()
    for i in range(2):
        twin[i].wait()

    @pl.loop(0, 4)
    def _(n):
        side, at = n // 2, n % 2
        rows = jnp.concatenate([halo[0, side, at].reshape(B, 256), halo[1, side, at].reshape(B, 256)], axis=1)
        i = side * 6 + at
        node = (first + i - 2 + devices * 4) % (devices * 4)
        project(rows, w_qkv[1], wv_t[...], usable_of(node), keys, vals, bias, i)

    @pl.loop(0, 6)
    def _(n):
        meet(n // 2 + n // 3, (n + 1) // 2 + 4 * (n // 3))

    for k in ORDER:
        gather[k].wait_recv()
        part, _ = at_plane(k, -1)
        pair.append(remote(hubs.at[core, part], hubs.at[core, part], c_send.at[k], c_recv.at[k], me, other))
        pair[-1].start()
    for copy in pair:
        copy.wait()
    for copy in list(scatter.values()) + lines + spread + list(gather.values()) + near:
        copy.wait_send()


def near_attention(hub_ids, lists, counts, feat, w_qkv, mask):
    dma = pltpu.SemaphoreType.DMA
    return pl.pallas_call(
        near_kernel,
        out_shape=(jax.ShapeDtypeStruct((2, 16, 8, 16, 256), BF16),
                   jax.ShapeDtypeStruct((4, HEADS_HERE, B, B), BF16),
                   jax.ShapeDtypeStruct((4, HEADS_HERE, TALL, B), F32),
                   jax.ShapeDtypeStruct((4, HEADS_HERE, 1, B), F32)),
        in_specs=[SMEM, SMEM, SMEM, VMEM, VMEM, VMEM],
        out_specs=(VMEM, VMEM, VMEM, VMEM),
        scratch_shapes=[
            pltpu.VMEM((2, 2, 2, 16, 16, 256), BF16),
            pltpu.VMEM((16, 4, 16, 256), BF16),
            pltpu.VMEM((8, 16, 256), BF16),
            pltpu.VMEM((8, 16, 256), BF16),
            pltpu.VMEM((256, 512), BF16),
            pltpu.VMEM((8, B, B), BF16),
            pltpu.VMEM((8, HEADS_HERE, TALL, B), BF16),
            pltpu.VMEM((8, B, 128), F32),
            dma(()),
            dma((15,)), dma((15,)), dma((7,)), dma((7,)), dma((7,)), dma((7,)), dma((15,)), dma((15,)),
            dma((16,)), dma((16,)), dma((2,)), dma((2,)), dma((2,)), dma((2,)),
        ],
        compiler_params=pltpu.CompilerParams(collective_id=0, has_side_effects=True,
                                             vmem_limit_bytes=40 << 20),
        name="near",
    )(hub_ids, lists, counts, feat.reshape(4, 16, 16, 512), w_qkv, mask)


def hub_kernel(hub_ids, lists, counts, hubs, q_t, acc_in, top_in, w_qkv, mask, out,
               wv_t, keys, vals, bias, acc, top, att_t, cnt):
    for b in range(4):
        for i in range(8):
            cnt[b, i] = 0
        for j in range(1, 5):
            cnt[b, lists[b, j]] += jnp.where(j < counts[b], 1, 0)
    acc[...] = acc_in[...]
    top[...] = top_in[...]
    wv_t[...] = w_qkv[2].T

    @pl.loop(0, 8)
    def _(k):
        rows = jnp.concatenate([
            jnp.concatenate([hubs[c, p, k] for p in range(16)], axis=0) for c in range(2)], axis=1)
        usable = (mask[pl.ds(hub_ids[k], 1), :] > 0).astype(F32)
        project(rows, w_qkv[1], wv_t[...], usable, keys, vals, bias, k)

    @pl.loop(0, 4)
    def _(b):
        @pl.loop(0, 8)
        def _(k):
            times = cnt[b, k]

            @pl.when(times > 0)
            def _():
                attend(q_t, b, keys[k], vals.at[k], bias[k], times, acc, top)

        for h in range(HEADS_HERE):
            att_t[h * DH:(h + 1) * DH, :] = (acc[b, h, 0:DH, :] / acc[b, h, DH:DH + 1, :]).astype(BF16)
        out[pl.ds(pl.multiple_of(b * B, B), B), :] = att_t[...].T


def hub_attention(hub_ids, lists, counts, hubs, q_t, acc, top, w_qkv, mask):
    return pl.pallas_call(
        hub_kernel,
        out_shape=jax.ShapeDtypeStruct((1024, 256), BF16),
        in_specs=[SMEM, SMEM, SMEM] + [VMEM] * 6,
        out_specs=VMEM,
        scratch_shapes=[
            pltpu.VMEM((256, 512), BF16),
            pltpu.VMEM((8, B, B), BF16),
            pltpu.VMEM((8, HEADS_HERE, TALL, B), BF16),
            pltpu.VMEM((8, B, 128), F32),
            pltpu.VMEM((4, HEADS_HERE, TALL, B), F32),
            pltpu.VMEM((4, HEADS_HERE, 1, B), F32),
            pltpu.VMEM((B, B), BF16),
            pltpu.SMEM((4, 8), jnp.int32),
        ],
        compiler_params=pltpu.CompilerParams(vmem_limit_bytes=40 << 20),
        name="hub",
    )(hub_ids, lists, counts, hubs, q_t, acc, top, w_qkv, mask)


def body(features, w_qkv, w_out, key_lists, key_counts, node_mask, hub_ids):
    width = features.shape[1]
    me = lax.axis_index("head")
    swap = [(0, 1), (1, 0)]
    share = width // 2
    mask = node_mask.reshape(-1, B)
    w_mine = lax.dynamic_slice_in_dim(w_out, me * share, share, 1)
    w_sent = lax.dynamic_slice_in_dim(w_out, (1 - me) * share, share, 1)
    w_got = lax.ppermute(w_sent, "head", swap)
    hubs, q_t, acc, top = near_attention(hub_ids, key_lists, key_counts, features, w_qkv, mask)
    attended = hub_attention(hub_ids, key_lists, key_counts, hubs, q_t, acc, top, w_qkv, mask)
    theirs = lax.ppermute(attended, "head", swap)
    resid = lax.dynamic_slice_in_dim(features, me * share, share, 1)
    mixed = (jnp.dot(attended, w_mine, preferred_element_type=F32)
             + jnp.dot(theirs, w_got, preferred_element_type=F32) + resid.astype(F32))
    return mixed.astype(BF16)


def solution(mesh):
    placed = (P("blk", None), P(None, None, "head"), P("head", None), P("blk", None), P("blk"), P(), P())
    return jax.shard_map(body, mesh=mesh, in_specs=placed, out_specs=P("blk", "head"), check_vma=False)
```

```python
import functools

import jax
import jax.numpy as jnp
from jax import lax
from jax.experimental import pallas as pl
from jax.experimental.pallas import tpu as pltpu
from jax.sharding import PartitionSpec as P

F32 = jnp.float32
BF16 = jnp.bfloat16
HEADS_HERE, DH, B = 4, 64, 256
TALL = DH + 16
NT = (((1,), (1,)), ((), ()))
NEG = -1e30
MESH = pl.DeviceIdType.MESH
VMEM = pl.BlockSpec(memory_space=pltpu.VMEM)
SMEM = pl.BlockSpec(memory_space=pltpu.SMEM)
HBM = pl.BlockSpec(memory_space=pltpu.HBM)
ORDER = sorted(range(1, 16), key=lambda k: -(min(k // 4, 4 - k // 4) + min(k % 4, 4 - k % 4)))


def project(rows, wk, wv_t, usable, keys, vals, bias, i):
    keys[i] = jnp.dot(rows, wk, preferred_element_type=F32).astype(BF16)
    v_t = lax.dot_general(wv_t, rows, NT, preferred_element_type=F32).astype(BF16)
    tail = jnp.concatenate([usable, jnp.zeros((TALL - DH - 1, B), F32)], axis=0).astype(BF16)
    for h in range(HEADS_HERE):
        vals[i, h, 0:DH, :] = v_t[h * DH:(h + 1) * DH, :] * usable.astype(BF16)
        vals[i, h, DH:TALL, :] = tail
    bias[i] = jnp.broadcast_to((usable - 1.0) * 1e30, (128, B)).T


def attend(q_t, b, kb, vb, low, times, acc, top):
    low = low + jnp.where(times > 0, 0.0, NEG)
    low = jnp.concatenate([low, low], axis=1)
    scale = times.astype(F32)
    heads = range(HEADS_HERE)
    ss = [jnp.dot(kb, q_t[b, h], preferred_element_type=F32) for h in heads]
    ss = [s + low for s in ss]
    olds = [top[b, h] for h in heads]
    news = [jnp.maximum(o, jnp.max(s, axis=0, keepdims=True)) for o, s in zip(olds, ss)]
    ps = [jnp.exp(s - n).astype(BF16) for s, n in zip(ss, news)]
    got = [jnp.dot(vb[h], ps[h], preferred_element_type=F32) for h in heads]
    for h in heads:
        acc[b, h] = jnp.exp(olds[h] - news[h]) * acc[b, h] + scale * got[h]
        top[b, h] = news[h]


def near_kernel(hub_ids_at, lists_at, counts_at, feat_at, w_at, mask, hubs, q_t, acc, top,
                hub_ids, lists, counts, feat, w_qkv, marks,
                halo, plane, zsend, zrecv, wv_t, keys, vals, bias, local, mark_sem,
                p_send, p_recv, z_send, z_recv, g_send, g_recv, a_send, a_recv, b_send, b_recv,
                c_send, c_recv, n_send, n_recv, m_send, m_recv):
    me = lax.axis_index("blk")
    core = lax.axis_index("head")
    devices = lax.axis_size("blk")
    x, y, z = me // 32, (me // 8) % 4, me % 8
    mine = x * 4 + y
    columns = pl.ds(pl.multiple_of(core * 256, 256), 256)
    other = 1 - core
    after = (me + 1) % devices
    before = (me + devices - 1) % devices

    def at_plane(k, sign=1):
        xx, yy = (x + sign * (k // 4) + 4) % 4, (y + sign * (k % 4) + 4) % 4
        return xx * 4 + yy, xx * 32 + yy * 8 + z

    def at_line(k):
        zz = (z + k) % 8
        return zz, x * 32 + y * 8 + zz

    def remote(src, dst, send, recv, blk, head):
        return pltpu.make_async_remote_copy(src_ref=src, dst_ref=dst, send_sem=send, recv_sem=recv,
                                            device_id=(blk, head), device_id_type=MESH)

    barrier = pltpu.get_barrier_semaphore()

    def greet(blk, head):
        pl.semaphore_signal(barrier, inc=1, device_id=(blk, head), device_id_type=MESH)

    for k in ORDER:
        greet(at_plane(k)[1], core)
    for k in range(1, 8):
        greet(at_line(k)[1], core)
    greet(after, core)
    greet(before, core)
    greet(me, other)
    own = pltpu.make_async_copy(feat_at.at[:, mine, :, columns], plane.at[mine], local.at[0])
    loads = [pltpu.make_async_copy(w_at, w_qkv, local.at[1]),
             pltpu.make_async_copy(feat_at, feat, local.at[2]),
             pltpu.make_async_copy(hub_ids_at, hub_ids, local.at[3]),
             pltpu.make_async_copy(lists_at, lists, local.at[4]),
             pltpu.make_async_copy(counts_at, counts, local.at[5]),
             own]
    first = me * 4
    for i in range(8):
        node = (first + i - 2 + devices * 4) % (devices * 4)
        loads.append(pltpu.make_async_copy(mask.at[pl.ds(pl.multiple_of(node * B, B), B)], marks.at[i, 0],
                                           mark_sem.at[i]))
    for copy in loads:
        copy.start()
    for copy in loads:
        copy.wait()

    wv_t[...] = w_qkv[2].T
    row_head = lax.broadcasted_iota(jnp.int32, (B, B), 0) // DH
    acc[...] = jnp.zeros_like(acc)
    top[...] = jnp.full_like(top, NEG)

    def usable_of(i):
        return (marks[i] > 0).astype(F32)

    @pl.loop(0, 4)
    def _(b):
        rows = feat[b].reshape(B, 512)
        q = jnp.dot(rows, w_qkv[0], preferred_element_type=F32).astype(BF16)
        q = (q * jnp.asarray(DH ** -0.5, BF16)).T
        for h in range(HEADS_HERE):
            q_t[b, h] = jnp.where(row_head == h, q, jnp.zeros_like(q))
        project(rows, w_qkv[1], wv_t[...], usable_of(b + 2), keys, vals, bias, b + 2)

    def meet(b, i):
        times = jnp.int32(0)
        for j in [0] + list(range(5, 16)):
            hit = (lists[b, j] == first + i - 2) & (j < counts[b])
            times = times + jnp.where(hit, 1, 0)
        attend(q_t, b, keys[i], vals.at[i], bias[i], times, acc, top)

    pl.semaphore_wait(barrier, 25)

    scatter = {}
    for k in ORDER:
        part, blk = at_plane(k)
        scatter[k] = remote(feat_at.at[:, part, :, columns], plane.at[mine],
                            p_send.at[k - 1], p_recv.at[k - 1], blk, core)
        scatter[k].start()

    @pl.loop(0, 10)
    def _(n):
        b = (n + 1) // 3
        meet(b, b + 1 + (n + 1) % 3)

    for copy in scatter.values():
        copy.wait_recv()

    for k in range(8):
        zsend[k] = plane[lax.div(hub_ids[k], 32), lax.rem(hub_ids[k], 4)]
    lines = []
    for k in (4, 3, 5, 2, 6, 1, 7):
        zz, blk = at_line(k)
        lines.append(remote(zsend.at[zz], zrecv.at[z], z_send.at[k - 1], z_recv.at[k - 1], blk, core))
        lines[-1].start()
    zrecv[z] = zsend[z]

    @pl.loop(0, 4)
    def _(n):
        b = (n % 2) * 2 + n // 2
        meet(b, (b + 2) % 4 + 2)

    for copy in lines:
        copy.wait_recv()
    hubs[core, mine, z] = zrecv[lax.rem(lax.div(hub_ids[z], 4), 8)]
    spread = []
    for k in (4, 3, 5, 2, 6, 1, 7):
        zz, blk = at_line(k)
        spread.append(remote(hubs.at[core, mine, z], hubs.at[core, mine, z],
                             g_send.at[k - 1], g_recv.at[k - 1], blk, core))
        spread[-1].start()
    for copy in spread:
        copy.wait_recv()

    along = jnp.where(core == 0, y, x)
    across = jnp.where(core == 0, x, y)
    along_blk, across_blk = jnp.where(core == 0, 8, 32), jnp.where(core == 0, 32, 8)
    along_part, across_part = jnp.where(core == 0, 1, 4), jnp.where(core == 0, 4, 1)

    def part_of(da, db):
        return ((along + da + 4) % 4) * along_part + ((across + db + 4) % 4) * across_part

    def send_on(da):
        part = part_of(-da, 0)
        sent = []
        for db in (2, 1, 3):
            n = da * 3 + db - 1
            sent.append(remote(hubs.at[core, part], hubs.at[core, part], b_send.at[n], b_recv.at[n],
                               me + ((across + db) % 4 - across) * across_blk, core))
            sent[-1].start()
        pair.append(remote(hubs.at[core, part], hubs.at[core, part], c_send.at[da], c_recv.at[da], me, other))
        pair[-1].start()
        return sent

    pair = []
    gather = []
    for da in (2, 1, 3):
        gather.append(remote(hubs.at[core, mine], hubs.at[core, mine], a_send.at[da - 1], a_recv.at[da - 1],
                             me + ((along + da) % 4 - along) * along_blk, core))
        gather[-1].start()
    onward = {0: send_on(0)}
    near = [
        remote(feat_at.at[2:4, :, :, columns], halo.at[core, 0], n_send.at[0], n_recv.at[0], after, core),
        remote(feat_at.at[0:2, :, :, columns], halo.at[core, 1], n_send.at[1], n_recv.at[1], before, core),
    ]
    for copy in near:
        copy.start()
    for da, at in ((1, 1), (3, 2), (2, 0)):
        gather[at].wait_recv()
        onward[da] = send_on(da)
    twin = []
    for i in range(2):
        near[i].wait_recv()
        twin.append(remote(halo.at[core, i], halo.at[core, i], m_send.at[i], m_recv.at[i], me, other))
        twin[i].start()
    for i in range(2):
        twin[i].wait()

    @pl.loop(0, 4)
    def _(n):
        side, at = n // 2, n % 2
        rows = jnp.concatenate([halo[0, side, at].reshape(B, 256), halo[1, side, at].reshape(B, 256)], axis=1)
        i = side * 6 + at
        project(rows, w_qkv[1], wv_t[...], usable_of(i), keys, vals, bias, i)

    @pl.loop(0, 6)
    def _(n):
        meet(n // 2 + n // 3, (n + 1) // 2 + 4 * (n // 3))

    for da in (0, 1, 3, 2):
        for n, db in ((1, 1), (2, 3), (0, 2)):
            onward[da][n].wait_recv()
            part = part_of(-da, -db)
            at = 4 + da * 3 + db - 1
            pair.append(remote(hubs.at[core, part], hubs.at[core, part], c_send.at[at], c_recv.at[at], me, other))
            pair[-1].start()
    for copy in pair:
        copy.wait()
    for copy in list(scatter.values()) + lines + spread + gather + sum(onward.values(), []) + near:
        copy.wait_send()


def near_attention(hub_ids, lists, counts, feat, w_qkv, mask):
    dma = pltpu.SemaphoreType.DMA
    return pl.pallas_call(
        near_kernel,
        out_shape=(jax.ShapeDtypeStruct((2, 16, 8, 16, 256), BF16),
                   jax.ShapeDtypeStruct((4, HEADS_HERE, B, B), BF16),
                   jax.ShapeDtypeStruct((4, HEADS_HERE, TALL, B), F32),
                   jax.ShapeDtypeStruct((4, HEADS_HERE, 1, B), F32)),
        in_specs=[HBM] * 6,
        out_specs=(VMEM, VMEM, VMEM, VMEM),
        scratch_shapes=[
            pltpu.SMEM((8,), jnp.int32),
            pltpu.SMEM((4, 16), jnp.int32),
            pltpu.SMEM((4,), jnp.int32),
            pltpu.VMEM((4, 16, 16, 512), BF16),
            pltpu.VMEM((3, 512, 256), BF16),
            pltpu.VMEM((8, 1, B), jnp.int32),
            pltpu.VMEM((2, 2, 2, 16, 16, 256), BF16),
            pltpu.VMEM((16, 4, 16, 256), BF16),
            pltpu.VMEM((8, 16, 256), BF16),
            pltpu.VMEM((8, 16, 256), BF16),
            pltpu.VMEM((256, 512), BF16),
            pltpu.VMEM((8, B, B), BF16),
            pltpu.VMEM((8, HEADS_HERE, TALL, B), BF16),
            pltpu.VMEM((8, B, 128), F32),
            dma((6,)), dma((8,)),
            dma((15,)), dma((15,)), dma((7,)), dma((7,)), dma((7,)), dma((7,)), dma((3,)), dma((3,)),
            dma((12,)), dma((12,)),
            dma((16,)), dma((16,)), dma((2,)), dma((2,)), dma((2,)), dma((2,)),
        ],
        compiler_params=pltpu.CompilerParams(collective_id=0, has_side_effects=True,
                                             vmem_limit_bytes=40 << 20),
        name="near",
    )(*[pltpu.with_memory_space_constraint(a, pltpu.HBM)
        for a in (hub_ids, lists, counts, feat.reshape(4, 16, 16, 512), w_qkv, mask)])


def hub_kernel(hub_ids, lists, counts, hubs, q_t, acc_in, top_in, w_qkv, mask, out,
               marks, mark_sem, wv_t, keys, vals, bias, acc, top, att_t, cnt):
    loads = []
    for k in range(8):
        loads.append(pltpu.make_async_copy(mask.at[pl.ds(pl.multiple_of(hub_ids[k] * B, B), B)], marks.at[k, 0],
                                           mark_sem.at[k]))
        loads[k].start()
    for b in range(4):
        for i in range(8):
            cnt[b, i] = 0
        for j in range(1, 5):
            cnt[b, lists[b, j]] += jnp.where(j < counts[b], 1, 0)
    acc[...] = acc_in[...]
    top[...] = top_in[...]
    wv_t[...] = w_qkv[2].T
    for copy in loads:
        copy.wait()

    @pl.loop(0, 8)
    def _(k):
        rows = jnp.concatenate([
            jnp.concatenate([hubs[c, p, k] for p in range(16)], axis=0) for c in range(2)], axis=1)
        usable = (marks[k] > 0).astype(F32)
        project(rows, w_qkv[1], wv_t[...], usable, keys, vals, bias, k)

    @pl.loop(0, 4)
    def _(b):
        @pl.loop(0, 8)
        def _(k):
            times = cnt[b, k]

            @pl.when(times > 0)
            def _():
                attend(q_t, b, keys[k], vals.at[k], bias[k], times, acc, top)

        for h in range(HEADS_HERE):
            att_t[h * DH:(h + 1) * DH, :] = (acc[b, h, 0:DH, :] / acc[b, h, DH:DH + 1, :]).astype(BF16)
        out[pl.ds(pl.multiple_of(b * B, B), B), :] = att_t[...].T


def hub_attention(hub_ids, lists, counts, hubs, q_t, acc, top, w_qkv, mask):
    return pl.pallas_call(
        hub_kernel,
        out_shape=jax.ShapeDtypeStruct((1024, 256), BF16),
        in_specs=[SMEM, SMEM, SMEM] + [VMEM] * 5 + [HBM],
        out_specs=VMEM,
        scratch_shapes=[
            pltpu.VMEM((8, 1, B), jnp.int32),
            pltpu.SemaphoreType.DMA((8,)),
            pltpu.VMEM((256, 512), BF16),
            pltpu.VMEM((8, B, B), BF16),
            pltpu.VMEM((8, HEADS_HERE, TALL, B), BF16),
            pltpu.VMEM((8, B, 128), F32),
            pltpu.VMEM((4, HEADS_HERE, TALL, B), F32),
            pltpu.VMEM((4, HEADS_HERE, 1, B), F32),
            pltpu.VMEM((B, B), BF16),
            pltpu.SMEM((4, 8), jnp.int32),
        ],
        compiler_params=pltpu.CompilerParams(vmem_limit_bytes=40 << 20),
        name="hub",
    )(hub_ids, lists, counts, hubs, q_t, acc, top, w_qkv, mask)


def body(features, w_qkv, w_out, key_lists, key_counts, node_mask, hub_ids):
    width = features.shape[1]
    me = lax.axis_index("head")
    swap = [(0, 1), (1, 0)]
    share = width // 2
    mask = node_mask
    w_mine = lax.dynamic_slice_in_dim(w_out, me * share, share, 1)
    w_sent = lax.dynamic_slice_in_dim(w_out, (1 - me) * share, share, 1)
    w_got = lax.ppermute(w_sent, "head", swap)
    hubs, q_t, acc, top = near_attention(hub_ids, key_lists, key_counts, features, w_qkv, mask)
    attended = hub_attention(hub_ids, key_lists, key_counts, hubs, q_t, acc, top, w_qkv, mask)
    theirs = lax.ppermute(attended, "head", swap)
    resid = lax.dynamic_slice_in_dim(features, me * share, share, 1)
    mixed = (jnp.dot(attended, w_mine, preferred_element_type=F32)
             + jnp.dot(theirs, w_got, preferred_element_type=F32) + resid.astype(F32))
    return mixed.astype(BF16)


def solution(mesh):
    placed = (P("blk", None), P(None, None, "head"), P("head", None), P("blk", None), P("blk"), P(), P())
    return jax.shard_map(body, mesh=mesh, in_specs=placed, out_specs=P("blk", "head"), check_vma=False)
```

```python
import functools

import jax
import jax.numpy as jnp
from jax import lax
from jax.experimental import pallas as pl
from jax.experimental.pallas import tpu as pltpu
from jax.sharding import PartitionSpec as P

F32 = jnp.float32
BF16 = jnp.bfloat16
HEADS_HERE, DH, B = 4, 64, 256
TALL = DH + 16
NT = (((1,), (1,)), ((), ()))
NEG = -1e30
MESH = pl.DeviceIdType.MESH
VMEM = pl.BlockSpec(memory_space=pltpu.VMEM)
SMEM = pl.BlockSpec(memory_space=pltpu.SMEM)
HBM = pl.BlockSpec(memory_space=pltpu.HBM)
ORDER = sorted(range(1, 16), key=lambda k: -(min(k // 4, 4 - k // 4) + min(k % 4, 4 - k % 4)))


def project(rows, wk, wv_t, usable, keys, vals, bias, i):
    keys[i] = jnp.dot(rows, wk, preferred_element_type=F32).astype(BF16)
    v_t = lax.dot_general(wv_t, rows, NT, preferred_element_type=F32).astype(BF16)
    tail = jnp.concatenate([usable, jnp.zeros((TALL - DH - 1, B), F32)], axis=0).astype(BF16)
    for h in range(HEADS_HERE):
        vals[i, h, 0:DH, :] = v_t[h * DH:(h + 1) * DH, :] * usable.astype(BF16)
        vals[i, h, DH:TALL, :] = tail
    bias[i] = jnp.broadcast_to((usable - 1.0) * 1e30, (128, B)).T


def squares(rows):
    r = lax.broadcasted_iota(jnp.int32, (B, 128), 0) // DH
    pick = (r == lax.broadcasted_iota(jnp.int32, (B, 128), 1)).astype(BF16)
    rows = rows.astype(F32)
    return jnp.max(jnp.dot((rows * rows).astype(BF16), pick, preferred_element_type=F32), axis=0, keepdims=True)


def attend(q_t, b, kb, vb, low, times, acc, top):
    low = low + jnp.where(times > 0, 0.0, NEG)
    low = jnp.concatenate([low, low], axis=1)
    scale = times.astype(F32)
    heads = range(HEADS_HERE)
    ss = [jnp.dot(kb, q_t[b, h], preferred_element_type=F32) for h in heads]
    ss = [s + low for s in ss]
    olds = [top[b, h] for h in heads]
    news = [jnp.maximum(o, jnp.max(s, axis=0, keepdims=True)) for o, s in zip(olds, ss)]
    ps = [jnp.exp(s - n).astype(BF16) for s, n in zip(ss, news)]
    got = [jnp.dot(vb[h], ps[h], preferred_element_type=F32) for h in heads]
    for h in heads:
        acc[b, h] = jnp.exp(olds[h] - news[h]) * acc[b, h] + scale * got[h]
        top[b, h] = news[h]


def near_kernel(hub_ids_at, lists_at, counts_at, feat_at, w_at, mask, w_out, hubs, q_t, acc, top, norm, w_got,
                hub_ids, lists, counts, feat, w_qkv, marks,
                halo, plane, zsend, zrecv, wv_t, keys, vals, bias, local, mark_sem,
                p_send, p_recv, z_send, z_recv, g_send, g_recv, a_send, a_recv, b_send, b_recv,
                c_send, c_recv, n_send, n_recv, m_send, m_recv, w_send, w_recv):
    me = lax.axis_index("blk")
    core = lax.axis_index("head")
    devices = lax.axis_size("blk")
    x, y, z = me // 32, (me // 8) % 4, me % 8
    mine = x * 4 + y
    columns = pl.ds(pl.multiple_of(core * 256, 256), 256)
    other = 1 - core
    after = (me + 1) % devices
    before = (me + devices - 1) % devices

    def at_plane(k, sign=1):
        xx, yy = (x + sign * (k // 4) + 4) % 4, (y + sign * (k % 4) + 4) % 4
        return xx * 4 + yy, xx * 32 + yy * 8 + z

    def at_line(k):
        zz = (z + k) % 8
        return zz, x * 32 + y * 8 + zz

    def remote(src, dst, send, recv, blk, head):
        return pltpu.make_async_remote_copy(src_ref=src, dst_ref=dst, send_sem=send, recv_sem=recv,
                                            device_id=(blk, head), device_id_type=MESH)

    barrier = pltpu.get_barrier_semaphore()

    def greet(blk, head):
        pl.semaphore_signal(barrier, inc=1, device_id=(blk, head), device_id_type=MESH)

    for k in ORDER:
        greet(at_plane(k)[1], core)
    for k in range(1, 8):
        greet(at_line(k)[1], core)
    greet(after, core)
    greet(before, core)
    greet(me, other)
    own = pltpu.make_async_copy(feat_at.at[:, mine, :, columns], plane.at[mine], local.at[0])
    loads = [pltpu.make_async_copy(w_at, w_qkv, local.at[1]),
             pltpu.make_async_copy(feat_at, feat, local.at[2]),
             pltpu.make_async_copy(hub_ids_at, hub_ids, local.at[3]),
             pltpu.make_async_copy(lists_at, lists, local.at[4]),
             pltpu.make_async_copy(counts_at, counts, local.at[5]),
             own]
    first = me * 4
    for i in range(8):
        node = (first + i - 2 + devices * 4) % (devices * 4)
        loads.append(pltpu.make_async_copy(mask.at[pl.ds(pl.multiple_of(node * B, B), B)], marks.at[i, 0],
                                           mark_sem.at[i]))
    for copy in loads:
        copy.start()
    for copy in loads:
        copy.wait()

    wv_t[...] = w_qkv[2].T
    row_head = lax.broadcasted_iota(jnp.int32, (B, B), 0) // DH
    acc[...] = jnp.zeros_like(acc)
    top[...] = jnp.full_like(top, NEG)
    norm[...] = jnp.zeros_like(norm)

    def usable_of(i):
        return (marks[i] > 0).astype(F32)

    @pl.loop(0, 4)
    def _(b):
        rows = feat[b].reshape(B, 512)
        q = jnp.dot(rows, w_qkv[0], preferred_element_type=F32).astype(BF16)
        norm[...] = jnp.maximum(norm[...], squares(q))
        q = (q * jnp.asarray(DH ** -0.5, BF16)).T
        for h in range(HEADS_HERE):
            q_t[b, h] = jnp.where(row_head == h, q, jnp.zeros_like(q))
        project(rows, w_qkv[1], wv_t[...], usable_of(b + 2), keys, vals, bias, b + 2)

    def meet(b, i):
        times = jnp.int32(0)
        for j in [0] + list(range(5, 16)):
            hit = (lists[b, j] == first + i - 2) & (j < counts[b])
            times = times + jnp.where(hit, 1, 0)
        attend(q_t, b, keys[i], vals.at[i], bias[i], times, acc, top)

    pl.semaphore_wait(barrier, 25)

    scatter = {}
    for k in ORDER:
        part, blk = at_plane(k)
        scatter[k] = remote(feat_at.at[:, part, :, columns], plane.at[mine],
                            p_send.at[k - 1], p_recv.at[k - 1], blk, core)
        scatter[k].start()
    near = [
        remote(feat_at.at[2:4, :, :, columns], halo.at[core, 0], n_send.at[0], n_recv.at[0], after, core),
        remote(feat_at.at[0:2, :, :, columns], halo.at[core, 1], n_send.at[1], n_recv.at[1], before, core),
    ]
    for copy in near:
        copy.start()
    weights = remote(w_out.at[:, pl.ds(pl.multiple_of(other * 256, 256), 256)], w_got, w_send.at[0], w_recv.at[0],
                     me, other)
    weights.start()

    @pl.loop(0, 10)
    def _(n):
        b = (n + 1) // 3
        meet(b, b + 1 + (n + 1) % 3)

    for copy in scatter.values():
        copy.wait_recv()

    for k in range(8):
        zsend[k] = plane[lax.div(hub_ids[k], 32), lax.rem(hub_ids[k], 4)]
    lines = []
    for k in (4, 3, 5, 2, 6, 1, 7):
        zz, blk = at_line(k)
        lines.append(remote(zsend.at[zz], zrecv.at[z], z_send.at[k - 1], z_recv.at[k - 1], blk, core))
        lines[-1].start()
    zrecv[z] = zsend[z]

    @pl.loop(0, 4)
    def _(n):
        b = (n % 2) * 2 + n // 2
        meet(b, (b + 2) % 4 + 2)

    for copy in lines:
        copy.wait_recv()
    hubs[core, mine, z] = zrecv[lax.rem(lax.div(hub_ids[z], 4), 8)]
    spread = []
    for k in (4, 3, 5, 2, 6, 1, 7):
        zz, blk = at_line(k)
        spread.append(remote(hubs.at[core, mine, z], hubs.at[core, mine, z],
                             g_send.at[k - 1], g_recv.at[k - 1], blk, core))
        spread[-1].start()
    twin = []
    for i in range(2):
        near[i].wait_recv()
        twin.append(remote(halo.at[core, i], halo.at[core, i], m_send.at[i], m_recv.at[i], me, other))
        twin[i].start()
    for copy in spread:
        copy.wait_recv()

    along = jnp.where(core == 0, y, x)
    across = jnp.where(core == 0, x, y)
    along_blk, across_blk = jnp.where(core == 0, 8, 32), jnp.where(core == 0, 32, 8)
    along_part, across_part = jnp.where(core == 0, 1, 4), jnp.where(core == 0, 4, 1)

    def part_of(da, db):
        return ((along + da + 4) % 4) * along_part + ((across + db + 4) % 4) * across_part

    def send_on(da):
        part = part_of(-da, 0)
        sent = []
        for db in (2, 1, 3):
            n = da * 3 + db - 1
            sent.append(remote(hubs.at[core, part], hubs.at[core, part], b_send.at[n], b_recv.at[n],
                               me + ((across + db) % 4 - across) * across_blk, core))
            sent[-1].start()
        pair.append(remote(hubs.at[core, part], hubs.at[core, part], c_send.at[da], c_recv.at[da], me, other))
        pair[-1].start()
        return sent

    pair = []
    gather = []
    for da in (2, 1, 3):
        gather.append(remote(hubs.at[core, mine], hubs.at[core, mine], a_send.at[da - 1], a_recv.at[da - 1],
                             me + ((along + da) % 4 - along) * along_blk, core))
        gather[-1].start()
    onward = {0: send_on(0)}
    for da, at in ((1, 1), (3, 2), (2, 0)):
        gather[at].wait_recv()
        onward[da] = send_on(da)
    for copy in twin:
        copy.wait()

    @pl.loop(0, 4)
    def _(n):
        side, at = n // 2, n % 2
        rows = jnp.concatenate([halo[0, side, at].reshape(B, 256), halo[1, side, at].reshape(B, 256)], axis=1)
        i = side * 6 + at
        project(rows, w_qkv[1], wv_t[...], usable_of(i), keys, vals, bias, i)

    @pl.loop(0, 6)
    def _(n):
        meet(n // 2 + n // 3, (n + 1) // 2 + 4 * (n // 3))

    for da in (0, 1, 3, 2):
        for n, db in ((1, 1), (2, 3), (0, 2)):
            onward[da][n].wait_recv()
            part = part_of(-da, -db)
            at = 4 + da * 3 + db - 1
            pair.append(remote(hubs.at[core, part], hubs.at[core, part], c_send.at[at], c_recv.at[at], me, other))
            pair[-1].start()
    for copy in pair + [weights]:
        copy.wait()
    for copy in list(scatter.values()) + lines + spread + gather + sum(onward.values(), []) + near:
        copy.wait_send()


def near_attention(hub_ids, lists, counts, feat, w_qkv, mask, w_out):
    dma = pltpu.SemaphoreType.DMA
    return pl.pallas_call(
        near_kernel,
        out_shape=(jax.ShapeDtypeStruct((2, 16, 8, 16, 256), BF16),
                   jax.ShapeDtypeStruct((4, HEADS_HERE, B, B), BF16),
                   jax.ShapeDtypeStruct((4, HEADS_HERE, TALL, B), F32),
                   jax.ShapeDtypeStruct((4, HEADS_HERE, 1, B), F32),
                   jax.ShapeDtypeStruct((1, 128), F32),
                   jax.ShapeDtypeStruct((256, 256), BF16)),
        in_specs=[HBM] * 7,
        out_specs=(VMEM,) * 6,
        scratch_shapes=[
            pltpu.SMEM((8,), jnp.int32),
            pltpu.SMEM((4, 16), jnp.int32),
            pltpu.SMEM((4,), jnp.int32),
            pltpu.VMEM((4, 16, 16, 512), BF16),
            pltpu.VMEM((3, 512, 256), BF16),
            pltpu.VMEM((8, 1, B), jnp.int32),
            pltpu.VMEM((2, 2, 2, 16, 16, 256), BF16),
            pltpu.VMEM((16, 4, 16, 256), BF16),
            pltpu.VMEM((8, 16, 256), BF16),
            pltpu.VMEM((8, 16, 256), BF16),
            pltpu.VMEM((256, 512), BF16),
            pltpu.VMEM((8, B, B), BF16),
            pltpu.VMEM((8, HEADS_HERE, TALL, B), BF16),
            pltpu.VMEM((8, B, 128), F32),
            dma((6,)), dma((8,)),
            dma((15,)), dma((15,)), dma((7,)), dma((7,)), dma((7,)), dma((7,)), dma((3,)), dma((3,)),
            dma((12,)), dma((12,)),
            dma((16,)), dma((16,)), dma((2,)), dma((2,)), dma((2,)), dma((2,)), dma((1,)), dma((1,)),
        ],
        compiler_params=pltpu.CompilerParams(collective_id=0, has_side_effects=True,
                                             vmem_limit_bytes=40 << 20),
        name="near",
    )(*[pltpu.with_memory_space_constraint(a, pltpu.HBM)
        for a in (hub_ids, lists, counts, feat.reshape(4, 16, 16, 512), w_qkv, mask, w_out)])


def hub_kernel(hub_ids, lists, counts, hubs, q_t, acc_in, top_in, norm, w_qkv, mask, out, acc, top,
               marks, mark_sem, wv_t, keys, vals, bias, att_t, cnt):
    loads = []
    for k in range(8):
        loads.append(pltpu.make_async_copy(mask.at[pl.ds(pl.multiple_of(hub_ids[k] * B, B), B)], marks.at[k, 0],
                                           mark_sem.at[k]))
        loads[k].start()
    for b in range(4):
        for i in range(8):
            cnt[b, i] = 0
        for j in range(1, 5):
            cnt[b, lists[b, j]] += jnp.where(j < counts[b], 1, 0)
    wv_t[...] = w_qkv[2].T
    for copy in loads:
        copy.wait()

    def prepare(k, longest):
        rows = jnp.concatenate([
            jnp.concatenate([hubs[c, p, k] for p in range(16)], axis=0) for c in range(2)], axis=1)
        usable = (marks[k] > 0).astype(F32)
        project(rows, w_qkv[1], wv_t[...], usable, keys, vals, bias, k)
        return jnp.maximum(longest, squares(keys[k]))

    longest = lax.fori_loop(0, 8, prepare, jnp.zeros((1, 128), F32))
    reach = jnp.sqrt(jnp.max(longest * norm[...]) * 1.02) * DH ** -0.5 + jnp.max(jnp.abs(top[...]))
    close = reach <= 40.0
    heads = range(HEADS_HERE)

    def over_hubs(step):
        @pl.loop(0, 4)
        def _(b):
            @pl.loop(0, 8)
            def _(k):
                times = cnt[b, k]

                @pl.when(times > 0)
                def _():
                    step(b, k, times)

    @pl.when(close)
    def _():
        def step(b, k, times):
            kb = keys[k]
            scale = times.astype(F32)
            ss = [jnp.dot(kb, q_t[b, h], preferred_element_type=F32) for h in heads]
            ps = [jnp.exp(ss[h] - top[b, h]).astype(BF16) for h in heads]
            got = [jnp.dot(vals[k, h], ps[h], preferred_element_type=F32) for h in heads]
            for h in heads:
                acc[b, h] += scale * got[h]

        over_hubs(step)

    @pl.when(jnp.logical_not(close))
    def _():
        over_hubs(lambda b, k, times: attend(q_t, b, keys[k], vals.at[k], bias[k], times, acc, top))

    @pl.loop(0, 4)
    def _(b):
        for h in heads:
            att_t[h * DH:(h + 1) * DH, :] = (acc[b, h, 0:DH, :] * (1.0 / acc[b, h, DH:DH + 1, :])).astype(BF16)
        out[pl.ds(pl.multiple_of(b * B, B), B), :] = att_t[...].T


def hub_attention(hub_ids, lists, counts, hubs, q_t, acc, top, norm, w_qkv, mask):
    return pl.pallas_call(
        hub_kernel,
        out_shape=(jax.ShapeDtypeStruct((1024, 256), BF16),
                   jax.ShapeDtypeStruct(acc.shape, F32),
                   jax.ShapeDtypeStruct(top.shape, F32)),
        in_specs=[SMEM, SMEM, SMEM] + [VMEM] * 6 + [HBM],
        out_specs=(VMEM,) * 3,
        input_output_aliases={5: 1, 6: 2},
        scratch_shapes=[
            pltpu.VMEM((8, 1, B), jnp.int32),
            pltpu.SemaphoreType.DMA((8,)),
            pltpu.VMEM((256, 512), BF16),
            pltpu.VMEM((8, B, B), BF16),
            pltpu.VMEM((8, HEADS_HERE, TALL, B), BF16),
            pltpu.VMEM((8, B, 128), F32),
            pltpu.VMEM((B, B), BF16),
            pltpu.SMEM((4, 8), jnp.int32),
        ],
        compiler_params=pltpu.CompilerParams(vmem_limit_bytes=40 << 20),
        name="hub",
    )(hub_ids, lists, counts, hubs, q_t, acc, top, norm, w_qkv, mask)[0]


def body(features, w_qkv, w_out, key_lists, key_counts, node_mask, hub_ids):
    width = features.shape[1]
    me = lax.axis_index("head")
    share = width // 2
    mask = node_mask
    w_mine = lax.dynamic_slice_in_dim(w_out, me * share, share, 1)
    hubs, q_t, acc, top, norm, w_got = near_attention(hub_ids, key_lists, key_counts, features, w_qkv, mask, w_out)
    attended = hub_attention(hub_ids, key_lists, key_counts, hubs, q_t, acc, top, norm, w_qkv, mask)
    theirs = lax.ppermute(attended, "head", [(0, 1), (1, 0)])
    resid = lax.dynamic_slice_in_dim(features, me * share, share, 1)
    mixed = (jnp.dot(attended, w_mine, preferred_element_type=F32)
             + jnp.dot(theirs, w_got, preferred_element_type=F32) + resid.astype(F32))
    return mixed.astype(BF16)


def solution(mesh):
    placed = (P("blk", None), P(None, None, "head"), P("head", None), P("blk", None), P("blk"), P(), P())
    return jax.shard_map(body, mesh=mesh, in_specs=placed, out_specs=P("blk", "head"), check_vma=False)
```

```python
import functools

import jax
import jax.numpy as jnp
from jax import lax
from jax.experimental import pallas as pl
from jax.experimental.pallas import tpu as pltpu
from jax.sharding import PartitionSpec as P

F32 = jnp.float32
BF16 = jnp.bfloat16
HEADS_HERE, DH, B = 4, 64, 256
TALL = DH + 16
NT = (((1,), (1,)), ((), ()))
NEG = -1e30
EARLY = 6
MESH = pl.DeviceIdType.MESH
VMEM = pl.BlockSpec(memory_space=pltpu.VMEM)
SMEM = pl.BlockSpec(memory_space=pltpu.SMEM)
HBM = pl.BlockSpec(memory_space=pltpu.HBM)
ORDER = sorted(range(1, 16), key=lambda k: -(min(k // 4, 4 - k // 4) + min(k % 4, 4 - k % 4)))


def project(rows, wk, wv_t, usable, keys, vals, bias, i):
    keys[i] = jnp.dot(rows, wk, preferred_element_type=F32).astype(BF16)
    v_t = lax.dot_general(wv_t, rows, NT, preferred_element_type=F32).astype(BF16)
    tail = jnp.concatenate([usable, jnp.zeros((TALL - DH - 1, B), F32)], axis=0).astype(BF16)
    for h in range(HEADS_HERE):
        vals[i, h, 0:DH, :] = v_t[h * DH:(h + 1) * DH, :] * usable.astype(BF16)
        vals[i, h, DH:TALL, :] = tail
    bias[i] = jnp.broadcast_to((usable - 1.0) * 1e30, (128, B)).T


def squares(rows):
    r = lax.broadcasted_iota(jnp.int32, (B, 128), 0) // DH
    pick = (r == lax.broadcasted_iota(jnp.int32, (B, 128), 1)).astype(BF16)
    rows = rows.astype(F32)
    return jnp.max(jnp.dot((rows * rows).astype(BF16), pick, preferred_element_type=F32), axis=0, keepdims=True)


def attend(q_t, b, kb, vb, low, times, acc, top):
    low = low + jnp.where(times > 0, 0.0, NEG)
    low = jnp.concatenate([low, low], axis=1)
    scale = times.astype(F32)
    heads = range(HEADS_HERE)
    ss = [jnp.dot(kb, q_t[b, h], preferred_element_type=F32) for h in heads]
    ss = [s + low for s in ss]
    olds = [top[b, h] for h in heads]
    news = [jnp.maximum(o, jnp.max(s, axis=0, keepdims=True)) for o, s in zip(olds, ss)]
    ps = [jnp.exp(s - n).astype(BF16) for s, n in zip(ss, news)]
    got = [jnp.dot(vb[h], ps[h], preferred_element_type=F32) for h in heads]
    for h in heads:
        acc[b, h] = jnp.exp(olds[h] - news[h]) * acc[b, h] + scale * got[h]
        top[b, h] = news[h]


def near_kernel(hub_ids_at, lists_at, counts_at, feat_at, w_at, mask, w_out,
                hubs, q_t, acc, top, norm, w_got, wk, wv_t,
                hub_ids, lists, counts, feat, w_qkv, marks,
                halo, plane, zsend, zrecv, keys, vals, bias, local, mark_sem,
                p_send, p_recv, z_send, z_recv, g_send, g_recv, a_send, a_recv, b_send, b_recv,
                c_send, c_recv, n_send, n_recv, m_send, m_recv, w_send, w_recv):
    me = lax.axis_index("blk")
    core = lax.axis_index("head")
    devices = lax.axis_size("blk")
    x, y, z = me // 32, (me // 8) % 4, me % 8
    mine = x * 4 + y
    columns = pl.ds(pl.multiple_of(core * 256, 256), 256)
    other = 1 - core
    after = (me + 1) % devices
    before = (me + devices - 1) % devices

    def at_plane(k, sign=1):
        xx, yy = (x + sign * (k // 4) + 4) % 4, (y + sign * (k % 4) + 4) % 4
        return xx * 4 + yy, xx * 32 + yy * 8 + z

    def at_line(k):
        zz = (z + k) % 8
        return zz, x * 32 + y * 8 + zz

    def remote(src, dst, send, recv, blk, head):
        return pltpu.make_async_remote_copy(src_ref=src, dst_ref=dst, send_sem=send, recv_sem=recv,
                                            device_id=(blk, head), device_id_type=MESH)

    barrier = pltpu.get_barrier_semaphore()

    def greet(blk, head):
        pl.semaphore_signal(barrier, inc=1, device_id=(blk, head), device_id_type=MESH)

    for k in ORDER:
        greet(at_plane(k)[1], core)
    for k in range(1, 8):
        greet(at_line(k)[1], core)
    greet(after, core)
    greet(before, core)
    greet(me, other)
    own = pltpu.make_async_copy(feat_at.at[:, mine, :, columns], plane.at[mine], local.at[0])
    loads = [pltpu.make_async_copy(w_at, w_qkv, local.at[1]),
             pltpu.make_async_copy(feat_at, feat, local.at[2]),
             pltpu.make_async_copy(hub_ids_at, hub_ids, local.at[3]),
             pltpu.make_async_copy(lists_at, lists, local.at[4]),
             pltpu.make_async_copy(counts_at, counts, local.at[5]),
             own]
    first = me * 4
    for i in range(8):
        node = (first + i - 2 + devices * 4) % (devices * 4)
        loads.append(pltpu.make_async_copy(mask.at[pl.ds(pl.multiple_of(node * B, B), B)], marks.at[i, 0],
                                           mark_sem.at[i]))
    for copy in loads:
        copy.start()
    pl.semaphore_wait(barrier, 25)

    scatter = {}
    for k in ORDER:
        part, blk = at_plane(k)
        scatter[k] = remote(feat_at.at[:, part, :, columns], plane.at[mine],
                            p_send.at[k - 1], p_recv.at[k - 1], blk, core)
        scatter[k].start()
    near = [
        remote(feat_at.at[2:4, :, :, columns], halo.at[core, 0], n_send.at[0], n_recv.at[0], after, core),
        remote(feat_at.at[0:2, :, :, columns], halo.at[core, 1], n_send.at[1], n_recv.at[1], before, core),
    ]
    for copy in near:
        copy.start()
    weights = remote(w_out.at[:, pl.ds(pl.multiple_of(other * 256, 256), 256)], w_got, w_send.at[0], w_recv.at[0],
                     me, other)
    weights.start()

    for copy in loads:
        copy.wait()
    wk[...] = w_qkv[1]
    wv_t[...] = w_qkv[2].T
    row_head = lax.broadcasted_iota(jnp.int32, (B, B), 0) // DH
    acc[...] = jnp.zeros_like(acc)
    top[...] = jnp.full_like(top, NEG)
    norm[...] = jnp.zeros_like(norm)

    def usable_of(i):
        return (marks[i] > 0).astype(F32)

    @pl.loop(0, 4)
    def _(b):
        rows = feat[b].reshape(B, 512)
        q = jnp.dot(rows, w_qkv[0], preferred_element_type=F32).astype(BF16)
        norm[...] = jnp.maximum(norm[...], squares(q))
        q = (q * jnp.asarray(DH ** -0.5, BF16)).T
        for h in range(HEADS_HERE):
            q_t[b, h] = jnp.where(row_head == h, q, jnp.zeros_like(q))
        project(rows, w_qkv[1], wv_t[...], usable_of(b + 2), keys, vals, bias, b + 2)

    def meet(b, i):
        times = jnp.int32(0)
        for j in [0] + list(range(5, 16)):
            hit = (lists[b, j] == first + i - 2) & (j < counts[b])
            times = times + jnp.where(hit, 1, 0)
        attend(q_t, b, keys[i], vals.at[i], bias[i], times, acc, top)

    def close_pair(n):
        b = (n + 1) // 3
        meet(b, b + 1 + (n + 1) % 3)

    pl.loop(0, EARLY)(close_pair)

    for copy in scatter.values():
        copy.wait_recv()

    for k in range(8):
        zsend[k] = plane[lax.div(hub_ids[k], 32), lax.rem(hub_ids[k], 4)]
    lines = []
    for k in (4, 3, 5, 2, 6, 1, 7):
        zz, blk = at_line(k)
        lines.append(remote(zsend.at[zz], zrecv.at[z], z_send.at[k - 1], z_recv.at[k - 1], blk, core))
        lines[-1].start()
    zrecv[z] = zsend[z]

    pl.loop(EARLY, 10)(close_pair)
    for copy in lines:
        copy.wait_recv()
    hubs[core, mine, z] = zrecv[lax.rem(lax.div(hub_ids[z], 4), 8)]
    spread = []
    for k in (4, 3, 5, 2, 6, 1, 7):
        zz, blk = at_line(k)
        spread.append(remote(hubs.at[core, mine, z], hubs.at[core, mine, z],
                             g_send.at[k - 1], g_recv.at[k - 1], blk, core))
        spread[-1].start()
    @pl.loop(0, 4)
    def _(n):
        b = (n % 2) * 2 + n // 2
        meet(b, (b + 2) % 4 + 2)

    twin = []
    for i in range(2):
        near[i].wait_recv()
        twin.append(remote(halo.at[core, i], halo.at[core, i], m_send.at[i], m_recv.at[i], me, other))
        twin[i].start()
    for copy in spread:
        copy.wait_recv()

    along = jnp.where(core == 0, y, x)
    across = jnp.where(core == 0, x, y)
    along_blk, across_blk = jnp.where(core == 0, 8, 32), jnp.where(core == 0, 32, 8)
    along_part, across_part = jnp.where(core == 0, 1, 4), jnp.where(core == 0, 4, 1)

    def part_of(da, db):
        return ((along + da + 4) % 4) * along_part + ((across + db + 4) % 4) * across_part

    def send_on(da):
        part = part_of(-da, 0)
        sent = []
        for db in (2, 1, 3):
            n = da * 3 + db - 1
            sent.append(remote(hubs.at[core, part], hubs.at[core, part], b_send.at[n], b_recv.at[n],
                               me + ((across + db) % 4 - across) * across_blk, core))
            sent[-1].start()
        pair.append(remote(hubs.at[core, part], hubs.at[core, part], c_send.at[da], c_recv.at[da], me, other))
        pair[-1].start()
        return sent

    pair = []
    gather = []
    for da in (2, 1, 3):
        gather.append(remote(hubs.at[core, mine], hubs.at[core, mine], a_send.at[da - 1], a_recv.at[da - 1],
                             me + ((along + da) % 4 - along) * along_blk, core))
        gather[-1].start()
    onward = {0: send_on(0)}
    for da, at in ((1, 1), (3, 2), (2, 0)):
        gather[at].wait_recv()
        onward[da] = send_on(da)
    for copy in twin:
        copy.wait()

    @pl.loop(0, 4)
    def _(n):
        side, at = n // 2, n % 2
        rows = jnp.concatenate([halo[0, side, at].reshape(B, 256), halo[1, side, at].reshape(B, 256)], axis=1)
        i = side * 6 + at
        project(rows, w_qkv[1], wv_t[...], usable_of(i), keys, vals, bias, i)

    @pl.loop(0, 6)
    def _(n):
        meet(n // 2 + n // 3, (n + 1) // 2 + 4 * (n // 3))

    for da in (0, 1, 3, 2):
        for n, db in ((1, 1), (2, 3), (0, 2)):
            onward[da][n].wait_recv()
            part = part_of(-da, -db)
            at = 4 + da * 3 + db - 1
            pair.append(remote(hubs.at[core, part], hubs.at[core, part], c_send.at[at], c_recv.at[at], me, other))
            pair[-1].start()
    for copy in pair + [weights]:
        copy.wait()
    for copy in list(scatter.values()) + lines + spread + gather + sum(onward.values(), []) + near:
        copy.wait_send()


def near_attention(hub_ids, lists, counts, feat, w_qkv, mask, w_out):
    dma = pltpu.SemaphoreType.DMA
    return pl.pallas_call(
        near_kernel,
        out_shape=(jax.ShapeDtypeStruct((2, 16, 8, 16, 256), BF16),
                   jax.ShapeDtypeStruct((4, HEADS_HERE, B, B), BF16),
                   jax.ShapeDtypeStruct((4, HEADS_HERE, TALL, B), F32),
                   jax.ShapeDtypeStruct((4, HEADS_HERE, 1, B), F32),
                   jax.ShapeDtypeStruct((1, 128), F32),
                   jax.ShapeDtypeStruct((256, 256), BF16),
                   jax.ShapeDtypeStruct((512, 256), BF16),
                   jax.ShapeDtypeStruct((256, 512), BF16)),
        in_specs=[HBM] * 7,
        out_specs=(VMEM,) * 8,
        scratch_shapes=[
            pltpu.SMEM((8,), jnp.int32),
            pltpu.SMEM((4, 16), jnp.int32),
            pltpu.SMEM((4,), jnp.int32),
            pltpu.VMEM((4, 16, 16, 512), BF16),
            pltpu.VMEM((3, 512, 256), BF16),
            pltpu.VMEM((8, 1, B), jnp.int32),
            pltpu.VMEM((2, 2, 2, 16, 16, 256), BF16),
            pltpu.VMEM((16, 4, 16, 256), BF16),
            pltpu.VMEM((8, 16, 256), BF16),
            pltpu.VMEM((8, 16, 256), BF16),
            pltpu.VMEM((8, B, B), BF16),
            pltpu.VMEM((8, HEADS_HERE, TALL, B), BF16),
            pltpu.VMEM((8, B, 128), F32),
            dma((6,)), dma((8,)),
            dma((15,)), dma((15,)), dma((7,)), dma((7,)), dma((7,)), dma((7,)), dma((3,)), dma((3,)),
            dma((12,)), dma((12,)),
            dma((16,)), dma((16,)), dma((2,)), dma((2,)), dma((2,)), dma((2,)), dma((1,)), dma((1,)),
        ],
        compiler_params=pltpu.CompilerParams(collective_id=0, has_side_effects=True,
                                             vmem_limit_bytes=40 << 20),
        name="near",
    )(*[pltpu.with_memory_space_constraint(a, pltpu.HBM)
        for a in (hub_ids, lists, counts, feat.reshape(4, 16, 16, 512), w_qkv, mask, w_out)])


def hub_kernel(hub_ids, lists, counts, hubs, q_t, acc_in, top_in, norm, wk, wv_t, mask, out, acc, top,
               marks, mark_sem, keys, vals, bias, att_t, cnt):
    loads = []
    for k in range(8):
        loads.append(pltpu.make_async_copy(mask.at[pl.ds(pl.multiple_of(hub_ids[k] * B, B), B)], marks.at[k, 0],
                                           mark_sem.at[k]))
        loads[k].start()
    for b in range(4):
        for i in range(8):
            cnt[b, i] = 0
        for j in range(1, 5):
            cnt[b, lists[b, j]] += jnp.where(j < counts[b], 1, 0)
    longest = jnp.zeros((1, 128), F32)
    for k in range(8):
        rows = jnp.concatenate([
            jnp.concatenate([hubs[c, p, k] for p in range(16)], axis=0) for c in range(2)], axis=1)
        loads[k].wait()
        usable = (marks[k] > 0).astype(F32)
        project(rows, wk[...], wv_t[...], usable, keys, vals, bias, k)
        longest = jnp.maximum(longest, squares(keys[k]))
    reach = jnp.sqrt(jnp.max(longest * norm[...]) * 1.02) * DH ** -0.5 + jnp.max(jnp.abs(top[...]))
    close = reach <= 40.0
    heads = range(HEADS_HERE)

    def over_hubs(step):
        @pl.loop(0, 4)
        def _(b):
            @pl.loop(0, 8)
            def _(k):
                times = cnt[b, k]

                @pl.when(times > 0)
                def _():
                    step(b, k, times)

    @pl.when(close)
    def _():
        def step(b, k, times):
            kb = keys[k]
            scale = times.astype(F32)
            ss = [jnp.dot(kb, q_t[b, h], preferred_element_type=F32) for h in heads]
            ps = [jnp.exp(ss[h] - top[b, h]).astype(BF16) for h in heads]
            got = [jnp.dot(vals[k, h], ps[h], preferred_element_type=F32) for h in heads]
            for h in heads:
                acc[b, h] += scale * got[h]

        over_hubs(step)

    @pl.when(jnp.logical_not(close))
    def _():
        over_hubs(lambda b, k, times: attend(q_t, b, keys[k], vals.at[k], bias[k], times, acc, top))

    @pl.loop(0, 4)
    def _(b):
        for h in heads:
            att_t[h * DH:(h + 1) * DH, :] = (acc[b, h, 0:DH, :] * (1.0 / acc[b, h, DH:DH + 1, :])).astype(BF16)
        out[pl.ds(pl.multiple_of(b * B, B), B), :] = att_t[...].T


def hub_attention(hub_ids, lists, counts, hubs, q_t, acc, top, norm, wk, wv_t, mask):
    return pl.pallas_call(
        hub_kernel,
        out_shape=(jax.ShapeDtypeStruct((1024, 256), BF16),
                   jax.ShapeDtypeStruct(acc.shape, F32),
                   jax.ShapeDtypeStruct(top.shape, F32)),
        in_specs=[SMEM, SMEM, SMEM] + [VMEM] * 7 + [HBM],
        out_specs=(VMEM,) * 3,
        input_output_aliases={5: 1, 6: 2},
        scratch_shapes=[
            pltpu.VMEM((8, 1, B), jnp.int32),
            pltpu.SemaphoreType.DMA((8,)),
            pltpu.VMEM((8, B, B), BF16),
            pltpu.VMEM((8, HEADS_HERE, TALL, B), BF16),
            pltpu.VMEM((8, B, 128), F32),
            pltpu.VMEM((B, B), BF16),
            pltpu.SMEM((4, 8), jnp.int32),
        ],
        compiler_params=pltpu.CompilerParams(vmem_limit_bytes=40 << 20),
        name="hub",
    )(hub_ids, lists, counts, hubs, q_t, acc, top, norm, wk, wv_t, mask)[0]


def body(features, w_qkv, w_out, key_lists, key_counts, node_mask, hub_ids):
    width = features.shape[1]
    me = lax.axis_index("head")
    share = width // 2
    mask = node_mask
    w_mine = lax.dynamic_slice_in_dim(w_out, me * share, share, 1)
    hubs, q_t, acc, top, norm, w_got, wk, wv_t = near_attention(
        hub_ids, key_lists, key_counts, features, w_qkv, mask, w_out)
    attended = hub_attention(hub_ids, key_lists, key_counts, hubs, q_t, acc, top, norm, wk, wv_t, mask)
    theirs = lax.ppermute(attended, "head", [(0, 1), (1, 0)])
    resid = lax.dynamic_slice_in_dim(features, me * share, share, 1)
    mixed = (jnp.dot(attended, w_mine, preferred_element_type=F32)
             + jnp.dot(theirs, w_got, preferred_element_type=F32) + resid.astype(F32))
    return mixed.astype(BF16)


def solution(mesh):
    placed = (P("blk", None), P(None, None, "head"), P("head", None), P("blk", None), P("blk"), P(), P())
    return jax.shard_map(body, mesh=mesh, in_specs=placed, out_specs=P("blk", "head"), check_vma=False)
```

```python
import functools

import jax
import jax.numpy as jnp
from jax import lax
from jax.experimental import pallas as pl
from jax.experimental.pallas import tpu as pltpu
from jax.sharding import PartitionSpec as P

F32 = jnp.float32
BF16 = jnp.bfloat16
HEADS_HERE, DH, B = 4, 64, 256
TALL = DH + 16
NT = (((1,), (1,)), ((), ()))
NEG = -1e30
EARLY = 6
MESH = pl.DeviceIdType.MESH
VMEM = pl.BlockSpec(memory_space=pltpu.VMEM)
SMEM = pl.BlockSpec(memory_space=pltpu.SMEM)
HBM = pl.BlockSpec(memory_space=pltpu.HBM)
ORDER = sorted(range(1, 16), key=lambda k: -(min(k // 4, 4 - k // 4) + min(k % 4, 4 - k % 4)))


def project(rows, wk, wv_t, usable, keys, vals, bias, i):
    keys[i] = jnp.dot(rows, wk, preferred_element_type=F32).astype(BF16)
    v_t = lax.dot_general(wv_t, rows, NT, preferred_element_type=F32).astype(BF16)
    tail = jnp.concatenate([usable, jnp.zeros((TALL - DH - 1, B), F32)], axis=0).astype(BF16)
    for h in range(HEADS_HERE):
        vals[i, h, 0:DH, :] = v_t[h * DH:(h + 1) * DH, :] * usable.astype(BF16)
        vals[i, h, DH:TALL, :] = tail
    bias[i] = jnp.broadcast_to((usable - 1.0) * 1e30, (128, B)).T


def squares(rows):
    r = lax.broadcasted_iota(jnp.int32, (B, 128), 0) // DH
    pick = (r == lax.broadcasted_iota(jnp.int32, (B, 128), 1)).astype(BF16)
    rows = rows.astype(F32)
    return jnp.max(jnp.dot((rows * rows).astype(BF16), pick, preferred_element_type=F32), axis=0, keepdims=True)


def attend(q_t, b, kb, vb, low, times, acc, top):
    low = low + jnp.where(times > 0, 0.0, NEG)
    low = jnp.concatenate([low, low], axis=1)
    scale = times.astype(F32)
    heads = range(HEADS_HERE)
    ss = [jnp.dot(kb, q_t[b, h], preferred_element_type=F32) for h in heads]
    ss = [s + low for s in ss]
    olds = [top[b, h] for h in heads]
    news = [jnp.maximum(o, jnp.max(s, axis=0, keepdims=True)) for o, s in zip(olds, ss)]
    ps = [jnp.exp(s - n).astype(BF16) for s, n in zip(ss, news)]
    got = [jnp.dot(vb[h], ps[h], preferred_element_type=F32) for h in heads]
    for h in heads:
        acc[b, h] = jnp.exp(olds[h] - news[h]) * acc[b, h] + scale * got[h]
        top[b, h] = news[h]


def near_kernel(hub_ids_at, lists_at, counts_at, feat_at, w_at, mask, w_out,
                hubs, q_t, acc, top, norm, w_got, wk, wv_t,
                hub_ids, lists, counts, feat, w_qkv, marks,
                halo, plane, zsend, zrecv, keys, vals, bias, local, mark_sem,
                p_send, p_recv, z_send, z_recv, g_send, g_recv, a_send, a_recv, b_send, b_recv,
                c_send, c_recv, n_send, n_recv, m_send, m_recv, w_send, w_recv):
    me = lax.axis_index("blk")
    core = lax.axis_index("head")
    devices = lax.axis_size("blk")
    x, y, z = me // 32, (me // 8) % 4, me % 8
    mine = x * 4 + y
    columns = pl.ds(pl.multiple_of(core * 256, 256), 256)
    other = 1 - core
    after = (me + 1) % devices
    before = (me + devices - 1) % devices

    def at_plane(k, sign=1):
        xx, yy = (x + sign * (k // 4) + 4) % 4, (y + sign * (k % 4) + 4) % 4
        return xx * 4 + yy, xx * 32 + yy * 8 + z

    def at_line(k):
        zz = (z + k) % 8
        return zz, x * 32 + y * 8 + zz

    def remote(src, dst, send, recv, blk, head):
        return pltpu.make_async_remote_copy(src_ref=src, dst_ref=dst, send_sem=send, recv_sem=recv,
                                            device_id=(blk, head), device_id_type=MESH)

    barrier = pltpu.get_barrier_semaphore()

    def greet(blk, head):
        pl.semaphore_signal(barrier, inc=1, device_id=(blk, head), device_id_type=MESH)

    for k in ORDER:
        greet(at_plane(k)[1], core)
    for k in range(1, 8):
        greet(at_line(k)[1], core)
    greet(after, core)
    greet(before, core)
    greet(me, other)
    own = pltpu.make_async_copy(feat_at.at[:, mine, :, columns], plane.at[mine], local.at[0])
    loads = [pltpu.make_async_copy(w_at, w_qkv, local.at[1]),
             pltpu.make_async_copy(feat_at, feat, local.at[2]),
             pltpu.make_async_copy(hub_ids_at, hub_ids, local.at[3]),
             pltpu.make_async_copy(lists_at, lists, local.at[4]),
             pltpu.make_async_copy(counts_at, counts, local.at[5]),
             own]
    first = me * 4
    for i in range(8):
        node = (first + i - 2 + devices * 4) % (devices * 4)
        loads.append(pltpu.make_async_copy(mask.at[pl.ds(pl.multiple_of(node * B, B), B)], marks.at[i, 0],
                                           mark_sem.at[i]))
    for copy in loads:
        copy.start()
    pl.semaphore_wait(barrier, 25)

    scatter = {}
    for k in ORDER:
        part, blk = at_plane(k)
        scatter[k] = remote(feat_at.at[:, part, :, columns], plane.at[mine],
                            p_send.at[k - 1], p_recv.at[k - 1], blk, core)
        scatter[k].start()
    near = [
        remote(feat_at.at[2:4, :, :, columns], halo.at[core, 0], n_send.at[0], n_recv.at[0], after, core),
        remote(feat_at.at[0:2, :, :, columns], halo.at[core, 1], n_send.at[1], n_recv.at[1], before, core),
    ]
    weights = remote(w_out.at[:, pl.ds(pl.multiple_of(other * 256, 256), 256)], w_got, w_send.at[0], w_recv.at[0],
                     me, other)
    weights.start()

    for copy in loads:
        copy.wait()
    wk[...] = w_qkv[1]
    wv_t[...] = w_qkv[2].T
    row_head = lax.broadcasted_iota(jnp.int32, (B, B), 0) // DH
    acc[...] = jnp.zeros_like(acc)
    top[...] = jnp.full_like(top, NEG)
    norm[...] = jnp.zeros_like(norm)

    def usable_of(i):
        return (marks[i] > 0).astype(F32)

    @pl.loop(0, 4)
    def _(b):
        rows = feat[b].reshape(B, 512)
        q = jnp.dot(rows, w_qkv[0], preferred_element_type=F32).astype(BF16)
        norm[...] = jnp.maximum(norm[...], squares(q))
        q = (q * jnp.asarray(DH ** -0.5, BF16)).T
        for h in range(HEADS_HERE):
            q_t[b, h] = jnp.where(row_head == h, q, jnp.zeros_like(q))
        project(rows, w_qkv[1], wv_t[...], usable_of(b + 2), keys, vals, bias, b + 2)

    def meet(b, i):
        times = jnp.int32(0)
        for j in [0] + list(range(5, 16)):
            hit = (lists[b, j] == first + i - 2) & (j < counts[b])
            times = times + jnp.where(hit, 1, 0)
        attend(q_t, b, keys[i], vals.at[i], bias[i], times, acc, top)

    def close_pair(n):
        b = (n + 1) // 3
        meet(b, b + 1 + (n + 1) % 3)

    pl.loop(0, EARLY)(close_pair)

    for copy in scatter.values():
        copy.wait_recv()

    for k in range(8):
        zsend[k] = plane[lax.div(hub_ids[k], 32), lax.rem(hub_ids[k], 4)]
    lines = []
    for k in (4, 3, 5, 2, 6, 1, 7):
        zz, blk = at_line(k)
        lines.append(remote(zsend.at[zz], zrecv.at[z], z_send.at[k - 1], z_recv.at[k - 1], blk, core))
        lines[-1].start()
    zrecv[z] = zsend[z]
    for copy in near:
        copy.start()

    pl.loop(EARLY, 10)(close_pair)
    for copy in lines:
        copy.wait_recv()
    hubs[core, mine, z] = zrecv[lax.rem(lax.div(hub_ids[z], 4), 8)]
    spread = []
    for k in (4, 3, 5, 2, 6, 1, 7):
        zz, blk = at_line(k)
        spread.append(remote(hubs.at[core, mine, z], hubs.at[core, mine, z],
                             g_send.at[k - 1], g_recv.at[k - 1], blk, core))
        spread[-1].start()
    @pl.loop(0, 4)
    def _(n):
        b = (n % 2) * 2 + n // 2
        meet(b, (b + 2) % 4 + 2)

    twin = []
    for i in range(2):
        near[i].wait_recv()
        twin.append(remote(halo.at[core, i], halo.at[core, i], m_send.at[i], m_recv.at[i], me, other))
        twin[i].start()
    for copy in spread:
        copy.wait_recv()

    along = jnp.where(core == 0, y, x)
    across = jnp.where(core == 0, x, y)
    along_blk, across_blk = jnp.where(core == 0, 8, 32), jnp.where(core == 0, 32, 8)
    along_part, across_part = jnp.where(core == 0, 1, 4), jnp.where(core == 0, 4, 1)

    def part_of(da, db):
        return ((along + da + 4) % 4) * along_part + ((across + db + 4) % 4) * across_part

    def send_on(da):
        part = part_of(-da, 0)
        sent = []
        for db in (2, 1, 3):
            n = da * 3 + db - 1
            sent.append(remote(hubs.at[core, part], hubs.at[core, part], b_send.at[n], b_recv.at[n],
                               me + ((across + db) % 4 - across) * across_blk, core))
            sent[-1].start()
        pair.append(remote(hubs.at[core, part], hubs.at[core, part], c_send.at[da], c_recv.at[da], me, other))
        pair[-1].start()
        return sent

    pair = []
    gather = []
    for da in (2, 1, 3):
        gather.append(remote(hubs.at[core, mine], hubs.at[core, mine], a_send.at[da - 1], a_recv.at[da - 1],
                             me + ((along + da) % 4 - along) * along_blk, core))
        gather[-1].start()
    onward = {0: send_on(0)}
    for da, at in ((1, 1), (3, 2), (2, 0)):
        gather[at].wait_recv()
        onward[da] = send_on(da)
    for copy in twin:
        copy.wait()

    @pl.loop(0, 4)
    def _(n):
        side, at = n // 2, n % 2
        rows = jnp.concatenate([halo[0, side, at].reshape(B, 256), halo[1, side, at].reshape(B, 256)], axis=1)
        i = side * 6 + at
        project(rows, w_qkv[1], wv_t[...], usable_of(i), keys, vals, bias, i)

    @pl.loop(0, 6)
    def _(n):
        meet(n // 2 + n // 3, (n + 1) // 2 + 4 * (n // 3))

    for da in (0, 1, 3, 2):
        for n, db in ((1, 1), (2, 3), (0, 2)):
            onward[da][n].wait_recv()
            part = part_of(-da, -db)
            at = 4 + da * 3 + db - 1
            pair.append(remote(hubs.at[core, part], hubs.at[core, part], c_send.at[at], c_recv.at[at], me, other))
            pair[-1].start()
    for copy in pair + [weights]:
        copy.wait()
    for copy in list(scatter.values()) + lines + spread + gather + sum(onward.values(), []) + near:
        copy.wait_send()


def near_attention(hub_ids, lists, counts, feat, w_qkv, mask, w_out):
    dma = pltpu.SemaphoreType.DMA
    return pl.pallas_call(
        near_kernel,
        out_shape=(jax.ShapeDtypeStruct((2, 16, 8, 16, 256), BF16),
                   jax.ShapeDtypeStruct((4, HEADS_HERE, B, B), BF16),
                   jax.ShapeDtypeStruct((4, HEADS_HERE, TALL, B), F32),
                   jax.ShapeDtypeStruct((4, HEADS_HERE, 1, B), F32),
                   jax.ShapeDtypeStruct((1, 128), F32),
                   jax.ShapeDtypeStruct((256, 256), BF16),
                   jax.ShapeDtypeStruct((512, 256), BF16),
                   jax.ShapeDtypeStruct((256, 512), BF16)),
        in_specs=[HBM] * 7,
        out_specs=(VMEM,) * 8,
        scratch_shapes=[
            pltpu.SMEM((8,), jnp.int32),
            pltpu.SMEM((4, 16), jnp.int32),
            pltpu.SMEM((4,), jnp.int32),
            pltpu.VMEM((4, 16, 16, 512), BF16),
            pltpu.VMEM((3, 512, 256), BF16),
            pltpu.VMEM((8, 1, B), jnp.int32),
            pltpu.VMEM((2, 2, 2, 16, 16, 256), BF16),
            pltpu.VMEM((16, 4, 16, 256), BF16),
            pltpu.VMEM((8, 16, 256), BF16),
            pltpu.VMEM((8, 16, 256), BF16),
            pltpu.VMEM((8, B, B), BF16),
            pltpu.VMEM((8, HEADS_HERE, TALL, B), BF16),
            pltpu.VMEM((8, B, 128), F32),
            dma((6,)), dma((8,)),
            dma((15,)), dma((15,)), dma((7,)), dma((7,)), dma((7,)), dma((7,)), dma((3,)), dma((3,)),
            dma((12,)), dma((12,)),
            dma((16,)), dma((16,)), dma((2,)), dma((2,)), dma((2,)), dma((2,)), dma((1,)), dma((1,)),
        ],
        compiler_params=pltpu.CompilerParams(collective_id=0, has_side_effects=True,
                                             vmem_limit_bytes=40 << 20),
        name="near",
    )(*[pltpu.with_memory_space_constraint(a, pltpu.HBM)
        for a in (hub_ids, lists, counts, feat.reshape(4, 16, 16, 512), w_qkv, mask, w_out)])


def hub_kernel(hub_ids, lists, counts, hubs, q_t, acc_in, top_in, norm, wk, wv_t, mask, out, acc, top,
               marks, mark_sem, keys, vals, bias, att_t, cnt):
    loads = []
    for k in range(8):
        loads.append(pltpu.make_async_copy(mask.at[pl.ds(pl.multiple_of(hub_ids[k] * B, B), B)], marks.at[k, 0],
                                           mark_sem.at[k]))
        loads[k].start()
    for b in range(4):
        for i in range(8):
            cnt[b, i] = 0
        for j in range(1, 5):
            cnt[b, lists[b, j]] += jnp.where(j < counts[b], 1, 0)
    longest = jnp.zeros((1, 128), F32)
    for k in range(8):
        rows = jnp.concatenate([
            jnp.concatenate([hubs[c, p, k] for p in range(16)], axis=0) for c in range(2)], axis=1)
        loads[k].wait()
        usable = (marks[k] > 0).astype(F32)
        project(rows, wk[...], wv_t[...], usable, keys, vals, bias, k)
        longest = jnp.maximum(longest, squares(keys[k]))
    reach = jnp.sqrt(jnp.max(longest * norm[...]) * 1.02) * DH ** -0.5 + jnp.max(jnp.abs(top[...]))
    close = reach <= 40.0
    heads = range(HEADS_HERE)

    def over_hubs(step):
        @pl.loop(0, 4)
        def _(b):
            @pl.loop(0, 8)
            def _(k):
                times = cnt[b, k]

                @pl.when(times > 0)
                def _():
                    step(b, k, times)

    @pl.when(close)
    def _():
        def step(b, k, times):
            kb = keys[k]
            scale = times.astype(F32)
            ss = [jnp.dot(kb, q_t[b, h], preferred_element_type=F32) for h in heads]
            ps = [jnp.exp(ss[h] - top[b, h]).astype(BF16) for h in heads]
            got = [jnp.dot(vals[k, h], ps[h], preferred_element_type=F32) for h in heads]
            for h in heads:
                acc[b, h] += scale * got[h]

        over_hubs(step)

    @pl.when(jnp.logical_not(close))
    def _():
        over_hubs(lambda b, k, times: attend(q_t, b, keys[k], vals.at[k], bias[k], times, acc, top))

    @pl.loop(0, 4)
    def _(b):
        for h in heads:
            att_t[h * DH:(h + 1) * DH, :] = (acc[b, h, 0:DH, :] * (1.0 / acc[b, h, DH:DH + 1, :])).astype(BF16)
        out[pl.ds(pl.multiple_of(b * B, B), B), :] = att_t[...].T


def hub_attention(hub_ids, lists, counts, hubs, q_t, acc, top, norm, wk, wv_t, mask):
    return pl.pallas_call(
        hub_kernel,
        out_shape=(jax.ShapeDtypeStruct((1024, 256), BF16),
                   jax.ShapeDtypeStruct(acc.shape, F32),
                   jax.ShapeDtypeStruct(top.shape, F32)),
        in_specs=[SMEM, SMEM, SMEM] + [VMEM] * 7 + [HBM],
        out_specs=(VMEM,) * 3,
        input_output_aliases={5: 1, 6: 2},
        scratch_shapes=[
            pltpu.VMEM((8, 1, B), jnp.int32),
            pltpu.SemaphoreType.DMA((8,)),
            pltpu.VMEM((8, B, B), BF16),
            pltpu.VMEM((8, HEADS_HERE, TALL, B), BF16),
            pltpu.VMEM((8, B, 128), F32),
            pltpu.VMEM((B, B), BF16),
            pltpu.SMEM((4, 8), jnp.int32),
        ],
        compiler_params=pltpu.CompilerParams(vmem_limit_bytes=40 << 20),
        name="hub",
    )(hub_ids, lists, counts, hubs, q_t, acc, top, norm, wk, wv_t, mask)[0]


def body(features, w_qkv, w_out, key_lists, key_counts, node_mask, hub_ids):
    width = features.shape[1]
    me = lax.axis_index("head")
    share = width // 2
    mask = node_mask
    w_mine = lax.dynamic_slice_in_dim(w_out, me * share, share, 1)
    hubs, q_t, acc, top, norm, w_got, wk, wv_t = near_attention(
        hub_ids, key_lists, key_counts, features, w_qkv, mask, w_out)
    attended = hub_attention(hub_ids, key_lists, key_counts, hubs, q_t, acc, top, norm, wk, wv_t, mask)
    theirs = lax.ppermute(attended, "head", [(0, 1), (1, 0)])
    resid = lax.dynamic_slice_in_dim(features, me * share, share, 1)
    mixed = (jnp.dot(attended, w_mine, preferred_element_type=F32)
             + jnp.dot(theirs, w_got, preferred_element_type=F32) + resid.astype(F32))
    return mixed.astype(BF16)


def solution(mesh):
    placed = (P("blk", None), P(None, None, "head"), P("head", None), P("blk", None), P("blk"), P(), P())
    return jax.shard_map(body, mesh=mesh, in_specs=placed, out_specs=P("blk", "head"), check_vma=False)
```

```python
import functools

import jax
import jax.numpy as jnp
from jax import lax
from jax.experimental import pallas as pl
from jax.experimental.pallas import tpu as pltpu
from jax.sharding import PartitionSpec as P

F32 = jnp.float32
BF16 = jnp.bfloat16
HEADS_HERE, DH, B = 4, 64, 256
TALL = DH + 16
NT = (((1,), (1,)), ((), ()))
NEG = -1e30
EARLY = 6
MESH = pl.DeviceIdType.MESH
VMEM = pl.BlockSpec(memory_space=pltpu.VMEM)
SMEM = pl.BlockSpec(memory_space=pltpu.SMEM)
HBM = pl.BlockSpec(memory_space=pltpu.HBM)
ORDER = sorted(range(1, 16), key=lambda k: -(min(k // 4, 4 - k // 4) + min(k % 4, 4 - k % 4)))


def project(rows, wk, wv_t, usable, keys, vals, bias, i):
    keys[i] = jnp.dot(rows, wk, preferred_element_type=F32).astype(BF16)
    v_t = lax.dot_general(wv_t, rows, NT, preferred_element_type=F32).astype(BF16)
    tail = jnp.concatenate([usable, jnp.zeros((TALL - DH - 1, B), F32)], axis=0).astype(BF16)
    for h in range(HEADS_HERE):
        vals[i, h, 0:DH, :] = v_t[h * DH:(h + 1) * DH, :] * usable.astype(BF16)
        vals[i, h, DH:TALL, :] = tail
    bias[i] = jnp.broadcast_to((usable - 1.0) * 1e30, (128, B)).T


def squares(rows):
    r = lax.broadcasted_iota(jnp.int32, (B, 128), 0) // DH
    pick = (r == lax.broadcasted_iota(jnp.int32, (B, 128), 1)).astype(BF16)
    rows = rows.astype(F32)
    return jnp.max(jnp.dot((rows * rows).astype(BF16), pick, preferred_element_type=F32), axis=0, keepdims=True)


def attend(q_t, b, kb, vb, low, times, acc, top):
    low = low + jnp.where(times > 0, 0.0, NEG)
    low = jnp.concatenate([low, low], axis=1)
    scale = times.astype(F32)
    heads = range(HEADS_HERE)
    ss = [jnp.dot(kb, q_t[b, h], preferred_element_type=F32) for h in heads]
    ss = [s + low for s in ss]
    olds = [top[b, h] for h in heads]
    news = [jnp.maximum(o, jnp.max(s, axis=0, keepdims=True)) for o, s in zip(olds, ss)]
    ps = [jnp.exp(s - n).astype(BF16) for s, n in zip(ss, news)]
    got = [jnp.dot(vb[h], ps[h], preferred_element_type=F32) for h in heads]
    for h in heads:
        acc[b, h] = jnp.exp(olds[h] - news[h]) * acc[b, h] + scale * got[h]
        top[b, h] = news[h]


def near_kernel(hub_ids_at, lists_at, counts_at, feat_at, w_at, mask, w_out,
                hubs, q_t, acc, top, norm, w_got, wk, wv_t,
                hub_ids, lists, counts, feat, w_qkv, marks,
                halo, plane, zsend, zrecv, keys, vals, bias, local, mark_sem,
                p_send, p_recv, z_send, z_recv, g_send, g_recv, a_send, a_recv, b_send, b_recv,
                c_send, c_recv, n_send, n_recv, m_send, m_recv, w_send, w_recv):
    me = lax.axis_index("blk")
    core = lax.axis_index("head")
    devices = lax.axis_size("blk")
    x, y, z = me // 32, (me // 8) % 4, me % 8
    mine = x * 4 + y
    columns = pl.ds(pl.multiple_of(core * 256, 256), 256)
    other = 1 - core
    after = (me + 1) % devices
    before = (me + devices - 1) % devices

    def at_plane(k, sign=1):
        xx, yy = (x + sign * (k // 4) + 4) % 4, (y + sign * (k % 4) + 4) % 4
        return xx * 4 + yy, xx * 32 + yy * 8 + z

    def at_line(k):
        zz = (z + k) % 8
        return zz, x * 32 + y * 8 + zz

    def remote(src, dst, send, recv, blk, head):
        return pltpu.make_async_remote_copy(src_ref=src, dst_ref=dst, send_sem=send, recv_sem=recv,
                                            device_id=(blk, head), device_id_type=MESH)

    barrier = pltpu.get_barrier_semaphore()

    def greet(blk, head):
        pl.semaphore_signal(barrier, inc=1, device_id=(blk, head), device_id_type=MESH)

    for k in ORDER:
        greet(at_plane(k)[1], core)
    for k in range(1, 8):
        greet(at_line(k)[1], core)
    greet(after, core)
    greet(before, core)
    greet(me, other)
    own = pltpu.make_async_copy(feat_at.at[:, mine, :, columns], plane.at[mine], local.at[0])
    loads = [pltpu.make_async_copy(w_at, w_qkv, local.at[1]),
             pltpu.make_async_copy(feat_at, feat, local.at[2]),
             pltpu.make_async_copy(hub_ids_at, hub_ids, local.at[3]),
             pltpu.make_async_copy(lists_at, lists, local.at[4]),
             pltpu.make_async_copy(counts_at, counts, local.at[5]),
             own]
    first = me * 4
    for i in range(8):
        node = (first + i - 2 + devices * 4) % (devices * 4)
        loads.append(pltpu.make_async_copy(mask.at[pl.ds(pl.multiple_of(node * B, B), B)], marks.at[i, 0],
                                           mark_sem.at[i]))
    for copy in loads:
        copy.start()
    pl.semaphore_wait(barrier, 25)

    scatter = {}
    for k in ORDER:
        part, blk = at_plane(k)
        scatter[k] = remote(feat_at.at[:, part, :, columns], plane.at[mine],
                            p_send.at[k - 1], p_recv.at[k - 1], blk, core)
        scatter[k].start()
    near = [
        remote(feat_at.at[2:4, :, :, columns], halo.at[core, 0], n_send.at[0], n_recv.at[0], after, core),
        remote(feat_at.at[0:2, :, :, columns], halo.at[core, 1], n_send.at[1], n_recv.at[1], before, core),
    ]
    weights = remote(w_out.at[:, pl.ds(pl.multiple_of(other * 256, 256), 256)], w_got, w_send.at[0], w_recv.at[0],
                     me, other)
    weights.start()

    for copy in loads:
        copy.wait()
    wk[...] = w_qkv[1]
    wv_t[...] = w_qkv[2].T
    row_head = lax.broadcasted_iota(jnp.int32, (B, B), 0) // DH
    acc[...] = jnp.zeros_like(acc)
    top[...] = jnp.full_like(top, NEG)
    norm[...] = jnp.zeros_like(norm)

    def usable_of(i):
        return (marks[i] > 0).astype(F32)

    @pl.loop(0, 4)
    def _(b):
        rows = feat[b].reshape(B, 512)
        q = jnp.dot(rows, w_qkv[0], preferred_element_type=F32).astype(BF16)
        norm[...] = jnp.maximum(norm[...], squares(q))
        q = (q * jnp.asarray(DH ** -0.5, BF16)).T
        for h in range(HEADS_HERE):
            q_t[b, h] = jnp.where(row_head == h, q, jnp.zeros_like(q))
        project(rows, w_qkv[1], wv_t[...], usable_of(b + 2), keys, vals, bias, b + 2)

    def meet(b, i):
        times = jnp.int32(0)
        for j in [0] + list(range(5, 16)):
            hit = (lists[b, j] == first + i - 2) & (j < counts[b])
            times = times + jnp.where(hit, 1, 0)
        attend(q_t, b, keys[i], vals.at[i], bias[i], times, acc, top)

    def close_pair(n):
        b = (n + 1) // 3
        meet(b, b + 1 + (n + 1) % 3)

    pl.loop(0, EARLY)(close_pair)

    for copy in scatter.values():
        copy.wait_recv()

    for k in range(8):
        zsend[k] = plane[lax.div(hub_ids[k], 32), lax.rem(hub_ids[k], 4)]
    lines = []
    for k in (4, 3, 5, 2, 6, 1, 7):
        zz, blk = at_line(k)
        lines.append(remote(zsend.at[zz], zrecv.at[z], z_send.at[k - 1], z_recv.at[k - 1], blk, core))
        lines[-1].start()
    zrecv[z] = zsend[z]
    for copy in near:
        copy.start()

    pl.loop(EARLY, 10)(close_pair)
    for copy in lines:
        copy.wait_recv()
    hubs[core, mine, z] = zrecv[lax.rem(lax.div(hub_ids[z], 4), 8)]
    spread = []
    for k in (4, 3, 5, 2, 6, 1, 7):
        zz, blk = at_line(k)
        spread.append(remote(hubs.at[core, mine, z], hubs.at[core, mine, z],
                             g_send.at[k - 1], g_recv.at[k - 1], blk, core))
        spread[-1].start()
    @pl.loop(0, 4)
    def _(n):
        b = (n % 2) * 2 + n // 2
        meet(b, (b + 2) % 4 + 2)

    twin = []
    for i in range(2):
        near[i].wait_recv()
        twin.append(remote(halo.at[core, i], halo.at[core, i], m_send.at[i], m_recv.at[i], me, other))
        twin[i].start()
    for copy in spread:
        copy.wait_recv()

    along = jnp.where(core == 0, y, x)
    across = jnp.where(core == 0, x, y)
    along_blk, across_blk = jnp.where(core == 0, 8, 32), jnp.where(core == 0, 32, 8)
    along_part, across_part = jnp.where(core == 0, 1, 4), jnp.where(core == 0, 4, 1)

    def part_of(da, db):
        return ((along + da + 4) % 4) * along_part + ((across + db + 4) % 4) * across_part

    def send_on(da):
        part = part_of(-da, 0)
        sent = []
        for db in (2, 1, 3):
            n = da * 3 + db - 1
            sent.append(remote(hubs.at[core, part], hubs.at[core, part], b_send.at[n], b_recv.at[n],
                               me + ((across + db) % 4 - across) * across_blk, core))
            sent[-1].start()
        pair.append(remote(hubs.at[core, part], hubs.at[core, part], c_send.at[da], c_recv.at[da], me, other))
        pair[-1].start()
        return sent

    pair = []
    gather = []
    for da in (2, 1, 3):
        gather.append(remote(hubs.at[core, mine], hubs.at[core, mine], a_send.at[da - 1], a_recv.at[da - 1],
                             me + ((along + da) % 4 - along) * along_blk, core))
        gather[-1].start()
    onward = {0: send_on(0)}
    for da, at in ((1, 1), (3, 2), (2, 0)):
        gather[at].wait_recv()
        onward[da] = send_on(da)
    for copy in twin:
        copy.wait()

    @pl.loop(0, 4)
    def _(n):
        side, at = n // 2, n % 2
        rows = jnp.concatenate([halo[0, side, at].reshape(B, 256), halo[1, side, at].reshape(B, 256)], axis=1)
        i = side * 6 + at
        project(rows, w_qkv[1], wv_t[...], usable_of(i), keys, vals, bias, i)

    @pl.loop(0, 6)
    def _(n):
        meet(n // 2 + n // 3, (n + 1) // 2 + 4 * (n // 3))

    for da in (0, 1, 3, 2):
        for n, db in ((1, 1), (2, 3), (0, 2)):
            onward[da][n].wait_recv()
            part = part_of(-da, -db)
            at = 4 + da * 3 + db - 1
            pair.append(remote(hubs.at[core, part], hubs.at[core, part], c_send.at[at], c_recv.at[at], me, other))
            pair[-1].start()
    for copy in pair + [weights]:
        copy.wait()
    for copy in list(scatter.values()) + lines + spread + gather + sum(onward.values(), []) + near:
        copy.wait_send()


def near_attention(hub_ids, lists, counts, feat, w_qkv, mask, w_out):
    dma = pltpu.SemaphoreType.DMA
    return pl.pallas_call(
        near_kernel,
        out_shape=(jax.ShapeDtypeStruct((2, 16, 8, 16, 256), BF16),
                   jax.ShapeDtypeStruct((4, HEADS_HERE, B, B), BF16),
                   jax.ShapeDtypeStruct((4, HEADS_HERE, TALL, B), F32),
                   jax.ShapeDtypeStruct((4, HEADS_HERE, 1, B), F32),
                   jax.ShapeDtypeStruct((1, 128), F32),
                   jax.ShapeDtypeStruct((256, 256), BF16),
                   jax.ShapeDtypeStruct((512, 256), BF16),
                   jax.ShapeDtypeStruct((256, 512), BF16)),
        in_specs=[HBM] * 7,
        out_specs=(VMEM,) * 8,
        scratch_shapes=[
            pltpu.SMEM((8,), jnp.int32),
            pltpu.SMEM((4, 16), jnp.int32),
            pltpu.SMEM((4,), jnp.int32),
            pltpu.VMEM((4, 16, 16, 512), BF16),
            pltpu.VMEM((3, 512, 256), BF16),
            pltpu.VMEM((8, 1, B), jnp.int32),
            pltpu.VMEM((2, 2, 2, 16, 16, 256), BF16),
            pltpu.VMEM((16, 4, 16, 256), BF16),
            pltpu.VMEM((8, 16, 256), BF16),
            pltpu.VMEM((8, 16, 256), BF16),
            pltpu.VMEM((8, B, B), BF16),
            pltpu.VMEM((8, HEADS_HERE, TALL, B), BF16),
            pltpu.VMEM((8, B, 128), F32),
            dma((6,)), dma((8,)),
            dma((15,)), dma((15,)), dma((7,)), dma((7,)), dma((7,)), dma((7,)), dma((3,)), dma((3,)),
            dma((12,)), dma((12,)),
            dma((16,)), dma((16,)), dma((2,)), dma((2,)), dma((2,)), dma((2,)), dma((1,)), dma((1,)),
        ],
        compiler_params=pltpu.CompilerParams(collective_id=0, has_side_effects=True,
                                             vmem_limit_bytes=40 << 20),
        name="near",
    )(*[pltpu.with_memory_space_constraint(a, pltpu.HBM)
        for a in (hub_ids, lists, counts, feat.reshape(4, 16, 16, 512), w_qkv, mask, w_out)])


def hub_kernel(hub_ids, lists, counts, hubs, q_t, acc_in, top_in, norm, wk, wv_t, mask, out, acc, top,
               marks, mark_sem, keys, vals, bias, att_t, cnt, named, length):
    loads = []
    for k in range(8):
        loads.append(pltpu.make_async_copy(mask.at[pl.ds(pl.multiple_of(hub_ids[k] * B, B), B)], marks.at[k, 0],
                                           mark_sem.at[k]))
        loads[k].start()
    for b in range(4):
        for i in range(8):
            cnt[b, i] = 0
        for j in range(1, 5):
            cnt[b, lists[b, j]] += jnp.where(j < counts[b], 1, 0)
        length[b] = 0
        for k in range(8):
            named[b, length[b]] = k
            length[b] += jnp.where(cnt[b, k] > 0, 1, 0)
    for copy in loads:
        copy.wait()
    longest = jnp.zeros((1, 128), F32)
    for k in range(8):
        rows = jnp.concatenate([
            jnp.concatenate([hubs[c, p, k] for p in range(16)], axis=0) for c in range(2)], axis=1)
        usable = (marks[k] > 0).astype(F32)
        project(rows, wk[...], wv_t[...], usable, keys, vals, bias, k)
        longest = jnp.maximum(longest, squares(keys[k]))
    reach = jnp.sqrt(jnp.max(longest * norm[...]) * 1.02) * DH ** -0.5 + jnp.max(jnp.abs(top[...]))
    close = reach <= 40.0
    heads = range(HEADS_HERE)

    def over_hubs(step):
        @pl.loop(0, 4)
        def _(b):
            @pl.loop(0, 8)
            def _(k):
                times = cnt[b, k]

                @pl.when(times > 0)
                def _():
                    step(b, k, times)

    @pl.when(close)
    def _():
        def step(b, *entries):
            which = [named[b, e] for e in entries]
            scales = [cnt[b, k].astype(F32) for k in which]
            kb = jnp.concatenate([keys[k] for k in which], axis=0)
            ss = [jnp.dot(kb, q_t[b, h], preferred_element_type=F32) for h in heads]
            ps = [jnp.exp(ss[h] - top[b, h]).astype(BF16) for h in heads]
            for h in heads:
                acc[b, h] += sum(
                    scale * jnp.dot(vals[k, h], ps[h][n * B:(n + 1) * B, :], preferred_element_type=F32)
                    for n, (k, scale) in enumerate(zip(which, scales)))

        @pl.loop(0, 4)
        def _(b):
            @pl.loop(0, length[b] // 2)
            def _(n):
                step(b, 2 * n, 2 * n + 1)

            @pl.when(length[b] % 2 == 1)
            def _():
                step(b, length[b] - 1)

    @pl.when(jnp.logical_not(close))
    def _():
        over_hubs(lambda b, k, times: attend(q_t, b, keys[k], vals.at[k], bias[k], times, acc, top))

    @pl.loop(0, 4)
    def _(b):
        for h in heads:
            att_t[h * DH:(h + 1) * DH, :] = (acc[b, h, 0:DH, :] * (1.0 / acc[b, h, DH:DH + 1, :])).astype(BF16)
        out[pl.ds(pl.multiple_of(b * B, B), B), :] = att_t[...].T


def hub_attention(hub_ids, lists, counts, hubs, q_t, acc, top, norm, wk, wv_t, mask):
    return pl.pallas_call(
        hub_kernel,
        out_shape=(jax.ShapeDtypeStruct((1024, 256), BF16),
                   jax.ShapeDtypeStruct(acc.shape, F32),
                   jax.ShapeDtypeStruct(top.shape, F32)),
        in_specs=[SMEM, SMEM, SMEM] + [VMEM] * 7 + [HBM],
        out_specs=(VMEM,) * 3,
        input_output_aliases={5: 1, 6: 2},
        scratch_shapes=[
            pltpu.VMEM((8, 1, B), jnp.int32),
            pltpu.SemaphoreType.DMA((8,)),
            pltpu.VMEM((8, B, B), BF16),
            pltpu.VMEM((8, HEADS_HERE, TALL, B), BF16),
            pltpu.VMEM((8, B, 128), F32),
            pltpu.VMEM((B, B), BF16),
            pltpu.SMEM((4, 8), jnp.int32),
            pltpu.SMEM((4, 8), jnp.int32),
            pltpu.SMEM((4,), jnp.int32),
        ],
        compiler_params=pltpu.CompilerParams(vmem_limit_bytes=40 << 20),
        name="hub",
    )(hub_ids, lists, counts, hubs, q_t, acc, top, norm, wk, wv_t, mask)[0]


def body(features, w_qkv, w_out, key_lists, key_counts, node_mask, hub_ids):
    width = features.shape[1]
    me = lax.axis_index("head")
    share = width // 2
    mask = node_mask
    w_mine = lax.dynamic_slice_in_dim(w_out, me * share, share, 1)
    hubs, q_t, acc, top, norm, w_got, wk, wv_t = near_attention(
        hub_ids, key_lists, key_counts, features, w_qkv, mask, w_out)
    attended = hub_attention(hub_ids, key_lists, key_counts, hubs, q_t, acc, top, norm, wk, wv_t, mask)
    theirs = lax.ppermute(attended, "head", [(0, 1), (1, 0)])
    resid = lax.dynamic_slice_in_dim(features, me * share, share, 1)
    mixed = (jnp.dot(attended, w_mine, preferred_element_type=F32)
             + jnp.dot(theirs, w_got, preferred_element_type=F32) + resid.astype(F32))
    return mixed.astype(BF16)


def solution(mesh):
    placed = (P("blk", None), P(None, None, "head"), P("head", None), P("blk", None), P("blk"), P(), P())
    return jax.shard_map(body, mesh=mesh, in_specs=placed, out_specs=P("blk", "head"), check_vma=False)
```

```python
import functools

import jax
import jax.numpy as jnp
from jax import lax
from jax.experimental import pallas as pl
from jax.experimental.pallas import tpu as pltpu
from jax.sharding import PartitionSpec as P

F32 = jnp.float32
BF16 = jnp.bfloat16
HEADS_HERE, DH, B = 4, 64, 256
TALL = DH + 16
NT = (((1,), (1,)), ((), ()))
NEG = -1e30
EARLY = 6
MESH = pl.DeviceIdType.MESH
VMEM = pl.BlockSpec(memory_space=pltpu.VMEM)
SMEM = pl.BlockSpec(memory_space=pltpu.SMEM)
HBM = pl.BlockSpec(memory_space=pltpu.HBM)
ORDER = sorted(range(1, 16), key=lambda k: -(min(k // 4, 4 - k // 4) + min(k % 4, 4 - k % 4)))


def project(rows, wk, wv_t, usable, keys, vals, bias, i):
    keys[i] = jnp.dot(rows, wk, preferred_element_type=F32).astype(BF16)
    v_t = lax.dot_general(wv_t, rows, NT, preferred_element_type=F32).astype(BF16)
    tail = jnp.concatenate([usable, jnp.zeros((TALL - DH - 1, B), F32)], axis=0).astype(BF16)
    for h in range(HEADS_HERE):
        vals[i, h, 0:DH, :] = v_t[h * DH:(h + 1) * DH, :] * usable.astype(BF16)
        vals[i, h, DH:TALL, :] = tail
    bias[i] = jnp.broadcast_to((usable - 1.0) * 1e30, (128, B)).T


def squares(rows):
    r = lax.broadcasted_iota(jnp.int32, (B, 128), 0) // DH
    pick = (r == lax.broadcasted_iota(jnp.int32, (B, 128), 1)).astype(BF16)
    rows = rows.astype(F32)
    return jnp.max(jnp.dot((rows * rows).astype(BF16), pick, preferred_element_type=F32), axis=0, keepdims=True)


def attend(q_t, b, kb, vb, low, times, acc, top):
    low = low + jnp.where(times > 0, 0.0, NEG)
    low = jnp.concatenate([low, low], axis=1)
    scale = times.astype(F32)
    heads = range(HEADS_HERE)
    ss = [jnp.dot(kb, q_t[b, h], preferred_element_type=F32) for h in heads]
    ss = [s + low for s in ss]
    olds = [top[b, h] for h in heads]
    news = [jnp.maximum(o, jnp.max(s, axis=0, keepdims=True)) for o, s in zip(olds, ss)]
    ps = [jnp.exp(s - n).astype(BF16) for s, n in zip(ss, news)]
    got = [jnp.dot(vb[h], ps[h], preferred_element_type=F32) for h in heads]
    for h in heads:
        acc[b, h] = jnp.exp(olds[h] - news[h]) * acc[b, h] + scale * got[h]
        top[b, h] = news[h]


def near_kernel(hub_ids_at, lists_at, counts_at, feat_at, w_at, mask, w_out,
                hubs, q_t, acc, top, norm, w_got, wk, wv_t,
                hub_ids, lists, counts, feat, w_qkv, marks,
                halo, plane, zsend, zrecv, keys, vals, bias, local, mark_sem,
                p_send, p_recv, z_send, z_recv, g_send, g_recv, a_send, a_recv, b_send, b_recv,
                c_send, c_recv, n_send, n_recv, m_send, m_recv, w_send, w_recv):
    me = lax.axis_index("blk")
    core = lax.axis_index("head")
    devices = lax.axis_size("blk")
    x, y, z = me // 32, (me // 8) % 4, me % 8
    mine = x * 4 + y
    columns = pl.ds(pl.multiple_of(core * 256, 256), 256)
    other = 1 - core
    after = (me + 1) % devices
    before = (me + devices - 1) % devices

    def at_plane(k, sign=1):
        xx, yy = (x + sign * (k // 4) + 4) % 4, (y + sign * (k % 4) + 4) % 4
        return xx * 4 + yy, xx * 32 + yy * 8 + z

    def at_line(k):
        zz = (z + k) % 8
        return zz, x * 32 + y * 8 + zz

    def remote(src, dst, send, recv, blk, head):
        return pltpu.make_async_remote_copy(src_ref=src, dst_ref=dst, send_sem=send, recv_sem=recv,
                                            device_id=(blk, head), device_id_type=MESH)

    barrier = pltpu.get_barrier_semaphore()

    def greet(blk, head):
        pl.semaphore_signal(barrier, inc=1, device_id=(blk, head), device_id_type=MESH)

    for k in ORDER:
        greet(at_plane(k)[1], core)
    for k in range(1, 8):
        greet(at_line(k)[1], core)
    greet(after, core)
    greet(before, core)
    greet(me, other)
    own = pltpu.make_async_copy(feat_at.at[:, mine, :, columns], plane.at[mine], local.at[0])
    loads = [pltpu.make_async_copy(w_at, w_qkv, local.at[1]),
             pltpu.make_async_copy(feat_at, feat, local.at[2]),
             pltpu.make_async_copy(hub_ids_at, hub_ids, local.at[3]),
             pltpu.make_async_copy(lists_at, lists, local.at[4]),
             pltpu.make_async_copy(counts_at, counts, local.at[5]),
             own]
    first = me * 4
    for i in range(8):
        node = (first + i - 2 + devices * 4) % (devices * 4)
        loads.append(pltpu.make_async_copy(mask.at[pl.ds(pl.multiple_of(node * B, B), B)], marks.at[i, 0],
                                           mark_sem.at[i]))
    for copy in loads:
        copy.start()
    pl.semaphore_wait(barrier, 25)

    scatter = {}
    for k in ORDER:
        part, blk = at_plane(k)
        scatter[k] = remote(feat_at.at[:, part, :, columns], plane.at[mine],
                            p_send.at[k - 1], p_recv.at[k - 1], blk, core)
        scatter[k].start()
    near = [
        remote(feat_at.at[2:4, :, :, columns], halo.at[core, 0], n_send.at[0], n_recv.at[0], after, core),
        remote(feat_at.at[0:2, :, :, columns], halo.at[core, 1], n_send.at[1], n_recv.at[1], before, core),
    ]
    weights = remote(w_out.at[:, pl.ds(pl.multiple_of(other * 256, 256), 256)], w_got, w_send.at[0], w_recv.at[0],
                     me, other)
    weights.start()

    for copy in loads:
        copy.wait()
    wk[...] = w_qkv[1]
    wv_t[...] = w_qkv[2].T
    row_head = lax.broadcasted_iota(jnp.int32, (B, B), 0) // DH
    acc[...] = jnp.zeros_like(acc)
    top[...] = jnp.full_like(top, NEG)
    norm[...] = jnp.zeros_like(norm)

    def usable_of(i):
        return (marks[i] > 0).astype(F32)

    @pl.loop(0, 4)
    def _(b):
        rows = feat[b].reshape(B, 512)
        q = jnp.dot(rows, w_qkv[0], preferred_element_type=F32).astype(BF16)
        norm[...] = jnp.maximum(norm[...], squares(q))
        q = (q * jnp.asarray(DH ** -0.5, BF16)).T
        for h in range(HEADS_HERE):
            q_t[b, h] = jnp.where(row_head == h, q, jnp.zeros_like(q))
        project(rows, w_qkv[1], wv_t[...], usable_of(b + 2), keys, vals, bias, b + 2)

    def meet(b, i):
        times = jnp.int32(0)
        for j in [0] + list(range(5, 16)):
            hit = (lists[b, j] == first + i - 2) & (j < counts[b])
            times = times + jnp.where(hit, 1, 0)
        attend(q_t, b, keys[i], vals.at[i], bias[i], times, acc, top)

    def close_pair(n):
        b = (n + 1) // 3
        meet(b, b + 1 + (n + 1) % 3)

    pl.loop(0, EARLY)(close_pair)

    for copy in scatter.values():
        copy.wait_recv()

    for k in range(8):
        zsend[k] = plane[lax.div(hub_ids[k], 32), lax.rem(hub_ids[k], 4)]
    lines = []
    for k in (4, 3, 5, 2, 6, 1, 7):
        zz, blk = at_line(k)
        lines.append(remote(zsend.at[zz], zrecv.at[z], z_send.at[k - 1], z_recv.at[k - 1], blk, core))
        lines[-1].start()
    zrecv[z] = zsend[z]
    for copy in near:
        copy.start()

    pl.loop(EARLY, 10)(close_pair)
    for copy in lines:
        copy.wait_recv()
    hubs[core, mine, z] = zrecv[lax.rem(lax.div(hub_ids[z], 4), 8)]
    spread = []
    for k in (4, 3, 5, 2, 6, 1, 7):
        zz, blk = at_line(k)
        spread.append(remote(hubs.at[core, mine, z], hubs.at[core, mine, z],
                             g_send.at[k - 1], g_recv.at[k - 1], blk, core))
        spread[-1].start()
    @pl.loop(0, 4)
    def _(n):
        b = (n % 2) * 2 + n // 2
        meet(b, (b + 2) % 4 + 2)

    twin = []
    for i in range(2):
        near[i].wait_recv()
        twin.append(remote(halo.at[core, i], halo.at[core, i], m_send.at[i], m_recv.at[i], me, other))
        twin[i].start()
    for copy in spread:
        copy.wait_recv()

    along = jnp.where(core == 0, y, x)
    across = jnp.where(core == 0, x, y)
    along_blk, across_blk = jnp.where(core == 0, 8, 32), jnp.where(core == 0, 32, 8)
    along_part, across_part = jnp.where(core == 0, 1, 4), jnp.where(core == 0, 4, 1)

    def part_of(da, db):
        return ((along + da + 4) % 4) * along_part + ((across + db + 4) % 4) * across_part

    def send_on(da):
        part = part_of(-da, 0)
        sent = []
        for db in (2, 1, 3):
            n = da * 3 + db - 1
            sent.append(remote(hubs.at[core, part], hubs.at[core, part], b_send.at[n], b_recv.at[n],
                               me + ((across + db) % 4 - across) * across_blk, core))
            sent[-1].start()
        pair.append(remote(hubs.at[core, part], hubs.at[core, part], c_send.at[da], c_recv.at[da], me, other))
        pair[-1].start()
        return sent

    pair = []
    gather = []
    for da in (2, 1, 3):
        gather.append(remote(hubs.at[core, mine], hubs.at[core, mine], a_send.at[da - 1], a_recv.at[da - 1],
                             me + ((along + da) % 4 - along) * along_blk, core))
        gather[-1].start()
    onward = {0: send_on(0)}
    for da, at in ((1, 1), (3, 2), (2, 0)):
        gather[at].wait_recv()
        onward[da] = send_on(da)
    for copy in twin:
        copy.wait()

    @pl.loop(0, 4)
    def _(n):
        side, at = n // 2, n % 2
        rows = jnp.concatenate([halo[0, side, at].reshape(B, 256), halo[1, side, at].reshape(B, 256)], axis=1)
        i = side * 6 + at
        project(rows, w_qkv[1], wv_t[...], usable_of(i), keys, vals, bias, i)

    @pl.loop(0, 6)
    def _(n):
        meet(n // 2 + n // 3, (n + 1) // 2 + 4 * (n // 3))

    for da in (0, 1, 3, 2):
        for n, db in ((1, 1), (2, 3), (0, 2)):
            onward[da][n].wait_recv()
            part = part_of(-da, -db)
            at = 4 + da * 3 + db - 1
            pair.append(remote(hubs.at[core, part], hubs.at[core, part], c_send.at[at], c_recv.at[at], me, other))
            pair[-1].start()
    for copy in pair + [weights]:
        copy.wait()
    for copy in list(scatter.values()) + lines + spread + gather + sum(onward.values(), []) + near:
        copy.wait_send()


def near_attention(hub_ids, lists, counts, feat, w_qkv, mask, w_out):
    dma = pltpu.SemaphoreType.DMA
    return pl.pallas_call(
        near_kernel,
        out_shape=(jax.ShapeDtypeStruct((2, 16, 8, 16, 256), BF16),
                   jax.ShapeDtypeStruct((4, HEADS_HERE, B, B), BF16),
                   jax.ShapeDtypeStruct((4, HEADS_HERE, TALL, B), F32),
                   jax.ShapeDtypeStruct((4, HEADS_HERE, 1, B), F32),
                   jax.ShapeDtypeStruct((1, 128), F32),
                   jax.ShapeDtypeStruct((256, 256), BF16),
                   jax.ShapeDtypeStruct((512, 256), BF16),
                   jax.ShapeDtypeStruct((256, 512), BF16)),
        in_specs=[HBM] * 7,
        out_specs=(VMEM,) * 8,
        scratch_shapes=[
            pltpu.SMEM((8,), jnp.int32),
            pltpu.SMEM((4, 16), jnp.int32),
            pltpu.SMEM((4,), jnp.int32),
            pltpu.VMEM((4, 16, 16, 512), BF16),
            pltpu.VMEM((3, 512, 256), BF16),
            pltpu.VMEM((8, 1, B), jnp.int32),
            pltpu.VMEM((2, 2, 2, 16, 16, 256), BF16),
            pltpu.VMEM((16, 4, 16, 256), BF16),
            pltpu.VMEM((8, 16, 256), BF16),
            pltpu.VMEM((8, 16, 256), BF16),
            pltpu.VMEM((8, B, B), BF16),
            pltpu.VMEM((8, HEADS_HERE, TALL, B), BF16),
            pltpu.VMEM((8, B, 128), F32),
            dma((6,)), dma((8,)),
            dma((15,)), dma((15,)), dma((7,)), dma((7,)), dma((7,)), dma((7,)), dma((3,)), dma((3,)),
            dma((12,)), dma((12,)),
            dma((16,)), dma((16,)), dma((2,)), dma((2,)), dma((2,)), dma((2,)), dma((1,)), dma((1,)),
        ],
        compiler_params=pltpu.CompilerParams(collective_id=0, has_side_effects=True,
                                             vmem_limit_bytes=40 << 20),
        name="near",
    )(*[pltpu.with_memory_space_constraint(a, pltpu.HBM)
        for a in (hub_ids, lists, counts, feat.reshape(4, 16, 16, 512), w_qkv, mask, w_out)])


def hub_kernel(hub_ids, lists, counts, hubs, q_t, acc_in, top_in, norm, wk, wv_t, mask, out, acc, top,
               marks, mark_sem, keys, vals, bias, att_t, cnt, named, length):
    loads = []
    for k in range(8):
        loads.append(pltpu.make_async_copy(mask.at[pl.ds(pl.multiple_of(hub_ids[k] * B, B), B)], marks.at[k, 0],
                                           mark_sem.at[k]))
        loads[k].start()
    for b in range(4):
        for i in range(8):
            cnt[b, i] = 0
        for j in range(1, 5):
            cnt[b, lists[b, j]] += jnp.where(j < counts[b], 1, 0)
        length[b] = 0
        for k in range(8):
            named[b, length[b]] = k
            length[b] += jnp.where(cnt[b, k] > 0, 1, 0)
    for copy in loads:
        copy.wait()
    longest = jnp.zeros((1, 128), F32)
    for k in range(8):
        rows = jnp.concatenate([
            jnp.concatenate([hubs[c, p, k] for p in range(16)], axis=0) for c in range(2)], axis=1)
        usable = (marks[k] > 0).astype(F32)
        project(rows, wk[...], wv_t[...], usable, keys, vals, bias, k)
        longest = jnp.maximum(longest, squares(keys[k]))
    reach = jnp.sqrt(jnp.max(longest * norm[...]) * 1.02) * DH ** -0.5 + jnp.max(jnp.abs(top[...]))
    close = reach <= 40.0
    heads = range(HEADS_HERE)

    def over_hubs(step):
        @pl.loop(0, 4)
        def _(b):
            @pl.loop(0, 8)
            def _(k):
                times = cnt[b, k]

                @pl.when(times > 0)
                def _():
                    step(b, k, times)

    @pl.when(close)
    def _():
        def step(b, *entries):
            which = [named[b, e] for e in entries]
            scales = [cnt[b, k].astype(F32) for k in which]
            kb = jnp.concatenate([keys[k] for k in which], axis=0)
            ss = [jnp.dot(kb, q_t[b, h], preferred_element_type=F32) for h in heads]
            ps = [jnp.exp(ss[h] - top[b, h]).astype(BF16) for h in heads]
            for h in heads:
                acc[b, h] += sum(
                    scale * jnp.dot(vals[k, h], ps[h][n * B:(n + 1) * B, :], preferred_element_type=F32)
                    for n, (k, scale) in enumerate(zip(which, scales)))

        @pl.loop(0, 4)
        def _(b):
            @pl.loop(0, length[b] // 2)
            def _(n):
                step(b, 2 * n, 2 * n + 1)

            @pl.when(length[b] % 2 == 1)
            def _():
                step(b, length[b] - 1)

    @pl.when(jnp.logical_not(close))
    def _():
        over_hubs(lambda b, k, times: attend(q_t, b, keys[k], vals.at[k], bias[k], times, acc, top))

    for b in range(4):
        for h in heads:
            att_t[b, h * DH:(h + 1) * DH, :] = (acc[b, h, 0:DH, :] * (1.0 / acc[b, h, DH:DH + 1, :])).astype(BF16)
        out[b * B:(b + 1) * B, :] = att_t[b].T


def hub_attention(hub_ids, lists, counts, hubs, q_t, acc, top, norm, wk, wv_t, mask):
    return pl.pallas_call(
        hub_kernel,
        out_shape=(jax.ShapeDtypeStruct((1024, 256), BF16),
                   jax.ShapeDtypeStruct(acc.shape, F32),
                   jax.ShapeDtypeStruct(top.shape, F32)),
        in_specs=[SMEM, SMEM, SMEM] + [VMEM] * 7 + [HBM],
        out_specs=(VMEM,) * 3,
        input_output_aliases={5: 1, 6: 2},
        scratch_shapes=[
            pltpu.VMEM((8, 1, B), jnp.int32),
            pltpu.SemaphoreType.DMA((8,)),
            pltpu.VMEM((8, B, B), BF16),
            pltpu.VMEM((8, HEADS_HERE, TALL, B), BF16),
            pltpu.VMEM((8, B, 128), F32),
            pltpu.VMEM((4, B, B), BF16),
            pltpu.SMEM((4, 8), jnp.int32),
            pltpu.SMEM((4, 8), jnp.int32),
            pltpu.SMEM((4,), jnp.int32),
        ],
        compiler_params=pltpu.CompilerParams(vmem_limit_bytes=40 << 20),
        name="hub",
    )(hub_ids, lists, counts, hubs, q_t, acc, top, norm, wk, wv_t, mask)[0]


def body(features, w_qkv, w_out, key_lists, key_counts, node_mask, hub_ids):
    width = features.shape[1]
    me = lax.axis_index("head")
    share = width // 2
    mask = node_mask
    w_mine = lax.dynamic_slice_in_dim(w_out, me * share, share, 1)
    hubs, q_t, acc, top, norm, w_got, wk, wv_t = near_attention(
        hub_ids, key_lists, key_counts, features, w_qkv, mask, w_out)
    attended = hub_attention(hub_ids, key_lists, key_counts, hubs, q_t, acc, top, norm, wk, wv_t, mask)
    theirs = lax.ppermute(attended, "head", [(0, 1), (1, 0)])
    resid = lax.dynamic_slice_in_dim(features, me * share, share, 1)
    mixed = (jnp.dot(attended, w_mine, preferred_element_type=F32)
             + jnp.dot(theirs, w_got, preferred_element_type=F32) + resid.astype(F32))
    return mixed.astype(BF16)


def solution(mesh):
    placed = (P("blk", None), P(None, None, "head"), P("head", None), P("blk", None), P("blk"), P(), P())
    return jax.shard_map(body, mesh=mesh, in_specs=placed, out_specs=P("blk", "head"), check_vma=False)
```
